32 devices in a mesh: survey: 2 (over x), freq: 16 (over z, y, core).
Axes of the slice: x: 2, y: 2, z: 4, core: 2. Of those that a mesh axis runs over, the one named last changes fastest.
Arguments:
- source: float32 [32, 2, 512, 512], P(('survey', 'freq')), parts along dimension 0, may hold values from -6 to 6
- receiver: float32 [32, 2, 512, 512], P(('survey', 'freq')), parts along dimension 0, may hold values from -6 to 6
- velocity: float32 [8, 512, 512], P('survey', 'freq'), parts along dimension 0, may hold values from 1.5 to 4.5
- anisotropy: float32 [8, 512, 512], P('survey', 'freq'), parts along dimension 0, may hold values from 0 to 0.3
- frequency: float32 [2], replicated, may hold values from 60 to 250
Outputs:
- image: float32 [8, 512, 512], P('survey', 'freq'), parts along dimension 0
The draws below stay inside these ranges and needn't reach their ends.
There are 2 independent parts, one for each index of `survey`. The reference program is written for one: setup_inputs(seed, part) draws one part's arguments, and reference() takes and returns one part's arrays. A program takes and returns all parts, laid end to end along the dimension named above; an argument that names none is the same for every part. Nothing has to cross between parts.
All inputs are finite; a program needn't handle non-finite values.
Results may differ from the reference program's by a relative error of at most 0.000029.
Values sent between devices are 32-bit elements; how exact they have to be, the bound alone decides.
No kernel may reach another device: no remote copies, remote signals or barrier semaphores. Data moves between devices by JAX's collectives and lax.ppermute only.
A program may use at most 128 MiB of HBM per device.

```python
import math
import jax
import jax.numpy as jnp
from jax import lax

NX = 512
NY = 512
DEPTH = 4
SWEEPS = 3
PAIRS = 16
FREQS = 2


def level_of(stream_key, shape, cuts, smallest, high):
    level, own = 1.0, jax.random.fold_in(stream_key, 6)
    for dim, shards_of in cuts:
        heights = jnp.exp(jax.random.uniform(jax.random.fold_in(own, dim), (shards_of,), jnp.float32, smallest / len(cuts), high / len(cuts)))
        level = level * jnp.repeat(heights, shape[dim] // shards_of).reshape([-1 if axis == dim else 1 for axis in range(len(shape))])
    return level


def scatter_about(rng, dims, width, most, cuts=(), kind=jnp.bfloat16):
    values = width * jax.random.normal(rng, dims, jnp.float32)
    if cuts:
        values = values * level_of(rng, dims, cuts, -0.22, 0.18)
    return jnp.clip(values, -most, most).astype(kind)


def setup_inputs(seed: int = 0, part: int = 0) -> dict:
    key_list = jax.random.split(jax.random.key(seed), 6)
    own_keys = jax.random.split(jax.random.fold_in(key_list[5], part), 6)
    return {
        "source": scatter_about(own_keys[0], (PAIRS, 2, NX, NY), 1.0, 6.0, ((0, 16),), jnp.float32),
        "receiver": scatter_about(own_keys[1], (PAIRS, 2, NX, NY), 1.0, 6.0, ((0, 16),), jnp.float32),
        "velocity": jnp.clip(1.5 + 3.0 * jax.random.uniform(own_keys[2], (DEPTH, NX, NY), jnp.float32) ** level_of(own_keys[2], (DEPTH, NX, NY), ((1, 16),), -0.2, 0.2), 1.5, 4.5),
        "anisotropy": jnp.clip(0.3 * jax.random.uniform(own_keys[3], (DEPTH, NX, NY), jnp.float32) ** level_of(own_keys[3], (DEPTH, NX, NY), ((1, 16),), -0.2, 0.2), 0.0, 0.3),
        "frequency": jnp.clip(jnp.exp(jax.random.uniform(key_list[4], (FREQS,), jnp.float32, math.log(60.0), math.log(250.0))), 60.0, 250.0),
    }


CENTER_WEIGHT = 10.0 / 3.0

def offlap(wavefield):
    widths = [(0, 0)] * (wavefield.ndim - 2) + [(1, 1), (1, 1)]
    padded = jnp.pad(wavefield, widths)
    edge_sum = padded[..., 2:, 1:-1] + padded[..., :-2, 1:-1] + padded[..., 1:-1, 2:] + padded[..., 1:-1, :-2]
    corner_sum = padded[..., 2:, 2:] + padded[..., 2:, :-2] + padded[..., :-2, 2:] + padded[..., :-2, :-2]
    return 2.0 / 3.0 * edge_sum + 1.0 / 6.0 * corner_sum

def extrapolate(real_part, imag_part, coef_map, phase_map, signed):
    cosine = jnp.cos(phase_map)
    sine = jnp.sin(phase_map) * signed
    shifted_real = real_part * cosine - imag_part * sine
    shifted_imag = imag_part * cosine + real_part * sine
    scaled = coef_map * signed
    lap_real = offlap(shifted_real) - CENTER_WEIGHT * shifted_real
    lap_imag = offlap(shifted_imag) - CENTER_WEIGHT * shifted_imag
    rhs_real = shifted_real - scaled * lap_imag
    rhs_imag = shifted_imag + scaled * lap_real
    damping = CENTER_WEIGHT * scaled
    denominator = 1.0 + damping * damping
    iterate_real, iterate_imag = (shifted_real, shifted_imag)
    for sweep_index in range(SWEEPS):
        numer_real = rhs_real - scaled * offlap(iterate_imag)
        numer_imag = rhs_imag + scaled * offlap(iterate_real)
        iterate_real = (numer_real + damping * numer_imag) / denominator
        iterate_imag = (numer_imag - damping * numer_real) / denominator
    return (iterate_real, iterate_imag)

def reference(source, receiver, velocity, anisotropy, frequency):
    pair_total = source.shape[0]
    freq_total = frequency.shape[0]
    pair_omega = jnp.tile(frequency, pair_total // freq_total)

    def one_pair(image_sum, inputs):
        src_field, rcv_field, omega = inputs
        src_real, src_imag = (src_field[0], src_field[1])
        rcv_real, rcv_imag = (rcv_field[0], rcv_field[1])
        layers = []
        for depth_step in range(DEPTH):
            slow_v = velocity[depth_step]
            coef_map = 6.0 * slow_v * (1.0 + 2.0 * anisotropy[depth_step]) / omega
            phase_map = 0.01 * omega / slow_v
            src_real, src_imag = extrapolate(src_real, src_imag, coef_map, phase_map, 1.0)
            rcv_real, rcv_imag = extrapolate(rcv_real, rcv_imag, coef_map, phase_map, -1.0)
            layers.append(src_real * rcv_real + src_imag * rcv_imag)
        return (image_sum + jnp.stack(layers), None)
    start = jnp.zeros((DEPTH,) + velocity.shape[1:], jnp.float32)
    image_sum, unused = lax.scan(one_pair, start, (source, receiver, pair_omega))
    return image_sum * (1.0 / math.sqrt(pair_total))
```

```python
import math
import numpy as np
import jax
import jax.numpy as jnp
from jax import lax
from jax.experimental import pallas as pl
from jax.experimental.pallas import tpu as pltpu
from jax.sharding import PartitionSpec as P


LANES = 128
SUB = 8
SIN_C = None
COS_C = None
TOP = 1.7


def even_fit(fun, degree):
    top = TOP * TOP
    nodes = 0.5 * top * (1.0 + np.cos(np.pi * (np.arange(degree + 1) + 0.5) / (degree + 1)))
    return [float(c) for c in np.polynomial.polynomial.polyfit(nodes, fun(np.sqrt(nodes)), degree)]


SIN_C = even_fit(lambda x: np.sin(x) / x, 5)
COS_C = even_fit(np.cos, 6)


def horner(coefs, z):
    acc = jnp.full_like(z, coefs[-1])
    acc = z * coefs[-1] + coefs[-2]
    for c in coefs[-3::-1]:
        acc = acc * z + c
    return acc


def kernel(cfg, me_ref, om_ref, *refs):
    first, last, n_blk, metas, U0, U1 = cfg["first"], cfg["last"], len(cfg["metas"]), cfg["metas"], cfg["U0"], cfg["U1"]
    refs = list(refs)
    blks = [refs.pop(0) for _ in range(n_blk)]
    if first:
        src, rcv = refs.pop(0), refs.pop(0)
    else:
        st_in = refs.pop(0)
    outs = [refs.pop(0) for _ in range(cfg["n_img"])]
    st = refs.pop(0)
    if not first:
        st_in_ref = st_in
    sh, e1, e2, mod, img, sem_m, sem_s, sem_o = refs
    G = mod.shape[1]
    NB = mod.shape[3] // LANES
    me_g, lo = me_ref[0], me_ref[1]
    R = cfg["R"]

    model_copies = []
    for ref, (k0, kb, other) in zip(blks, metas):
        base = (1 - lo) * R if other else lo * R
        for k in range(kb):
            for m in range(2):
                model_copies.append(pltpu.make_async_copy(
                    ref.at[k, m], mod.at[m, pl.ds(base, R), k0 + k, :], sem_m))
    for c in model_copies:
        c.start()
    state_copies = []
    if first:
        for k in range(SUB):
            off = ((k & 3) << 1) | (k >> 2)
            row = pl.multiple_of((me_g ^ off) * G, G)
            for a, ref in enumerate((src, rcv)):
                for c in range(2):
                    state_copies.append(pltpu.make_async_copy(
                        ref.at[c, pl.ds(row, G), :], st.at[2 * a + c, :, k, :], sem_s))
        for c in state_copies:
            c.start()
    cur = st if first else st_in_ref

    lane = lax.broadcasted_iota(jnp.int32, (SUB, LANES), 1)
    left_edge, right_edge = lane == 0, lane == LANES - 1
    kk = lax.broadcasted_iota(jnp.int32, (SUB, LANES), 0)
    g = me_g ^ (((kk & 3) << 1) | (kk >> 2))
    at = lambda g: ((lambda o: ((o & 1) << 2) | (o >> 1))(me_g ^ (g & 7)))
    up_idx, dn_idx = at(g - 1), at(g + 1)
    has_up, has_dn = g > 0, g < SUB - 1

    def cut(b):
        return slice(b * LANES, (b + 1) * LANES)

    def halos(buf):
        for c in range(4):
            for b in range(NB):
                v = buf[c, G, :, cut(b)]
                buf[c, 0, :, cut(b)] = jnp.where(has_up, jnp.take_along_axis(v, up_idx, axis=0), 0.0)
                v = buf[c, 1, :, cut(b)]
                buf[c, G + 1, :, cut(b)] = jnp.where(has_dn, jnp.take_along_axis(v, dn_idx, axis=0), 0.0)

    def around(up, mid, dn):
        r = [a + b for a, b in zip(up, dn)]
        t = [m + 0.25 * a for m, a in zip(mid, r)]
        a1 = [pltpu.roll(x, 1, 1) for x in t]
        a2 = [pltpu.roll(x, LANES - 1, 1) for x in t]
        out = []
        for b in range(NB):
            left = jnp.where(left_edge, a1[b - 1] if b else 0.0, a1[b])
            right = jnp.where(right_edge, a2[b + 1] if b < NB - 1 else 0.0, a2[b])
            out.append(r[b] + (left + right))
        return out

    om = om_ref[0]
    k1 = 6.0 / om
    kp = 0.01 * om
    for c in model_copies:
        c.wait()
    for c in state_copies:
        c.wait()

    def stage0(j, _):
        for q in range(U0):
            i = j * U0 + q
            for b in range(NB):
                v = mod[0, i, :, cut(b)]
                eta = mod[1, i, :, cut(b)]
                cf = (v * k1) * (1.0 + 2.0 * eta)
                d = cf * (10.0 / 3.0)
                den = 1.0 + d * d
                inv = 1.0 / (v * den)
                ph = kp * (den * inv)
                bi = (cf * (2.0 / 3.0)) * (v * inv)
                mod[0, i, :, cut(b)] = bi * d
                mod[1, i, :, cut(b)] = bi
                z = ph * ph
                sn = ph * horner(SIN_C, z)
                cs = horner(COS_C, z)
                for f in range(2):
                    re, im = cur[2 * f, i, :, cut(b)], cur[2 * f + 1, i, :, cut(b)]
                    if first and f == 1:
                        sh[2 * f, i + 1, :, cut(b)] = re * cs + im * sn
                        sh[2 * f + 1, i + 1, :, cut(b)] = re * sn - im * cs
                    else:
                        sh[2 * f, i + 1, :, cut(b)] = re * cs - im * sn
                        sh[2 * f + 1, i + 1, :, cut(b)] = im * cs + re * sn
        return 0
    lax.fori_loop(0, G // U0, stage0, 0)
    halos(sh)

    def sweep(src_buf, finish):
        def body(j, _):
            i0 = j * U1
            for f in range(2):
                rows = [[[src_buf[2 * f + c, i0 + q, :, cut(b)] for b in range(NB)] for q in range(U1 + 2)] for c in range(2)]
                for q in range(U1):
                    i = i0 + q
                    o = [around(rows[c][q], rows[c][q + 1], rows[c][q + 2]) for c in range(2)]
                    finish(f, i, o, [rows[c][q + 1] for c in range(2)])
            return 0
        lax.fori_loop(0, G // U1, body, 0)

    def times(i, b, x, y):
        br, bi = mod[0, i, :, cut(b)], mod[1, i, :, cut(b)]
        return br * x - bi * y, br * y + bi * x

    def fin1(f, i, o, mid):
        for b in range(NB):
            x, y = times(i, b, o[0][b] - 5.0 * mid[0][b], o[1][b] - 5.0 * mid[1][b])
            e1[2 * f, i + 1, :, cut(b)] = x
            e1[2 * f + 1, i + 1, :, cut(b)] = y
    sweep(sh, fin1)
    halos(e1)

    def fin2(f, i, o, mid):
        for b in range(NB):
            x, y = times(i, b, o[0][b], o[1][b])
            e2[2 * f, i + 1, :, cut(b)] = x
            e2[2 * f + 1, i + 1, :, cut(b)] = y
    sweep(e1, fin2)
    halos(e2)

    keep = {}
    def fin3(f, i, o, mid):
        for b in range(NB):
            x, y = times(i, b, o[0][b], o[1][b])
            new = []
            for c, x in enumerate((x, y)):
                total = (x + mid[c][b]) + e1[2 * f + c, i + 1, :, cut(b)]
                new.append(sh[2 * f + c, i + 1, :, cut(b)] + (total + total))
                if not last:
                    st[2 * f + c, i, :, cut(b)] = new[c]
            if last:
                if f == 0:
                    e1[0, i + 1, :, cut(b)] = new[0]
                    e1[1, i + 1, :, cut(b)] = new[1]
                else:
                    img[i, :, cut(b)] = e1[0, i + 1, :, cut(b)] * new[0] - e1[1, i + 1, :, cut(b)] * new[1]
            elif f == 1:
                img[i, :, cut(b)] = st[0, i, :, cut(b)] * new[0] - st[1, i, :, cut(b)] * new[1]
    sweep(e2, fin3)

    out_copies = []
    for o_i, out in enumerate(outs):
        base = lo * R if o_i == 0 else (1 - lo) * R
        for k in range(SUB):
            out_copies.append(pltpu.make_async_copy(img.at[pl.ds(base, R), k, :], out.at[k], sem_o))
    for c in out_copies:
        c.start()
    for c in out_copies:
        c.wait()


def depth_call(me, omega, blocks, metas, state, *, first, last, G, NY, n_img, U0=1, U1=2):
    R = G // n_img
    st_shape = jax.ShapeDtypeStruct((4, G, SUB, NY), jnp.float32)
    smem, vmem, anym = (pl.BlockSpec(memory_space=s) for s in (pltpu.SMEM, pltpu.VMEM, pl.ANY))
    cfg = dict(first=first, last=last, metas=metas, R=R, n_img=n_img, U0=U0, U1=U1)
    ins = [me, omega, *blocks, *(state if first else (state,))]
    in_specs = [smem, smem] + [anym] * len(blocks) + ([anym, anym] if first else [vmem])
    out_shape = [jax.ShapeDtypeStruct((SUB, R, NY), jnp.float32)] * n_img
    out_specs = [anym] * n_img
    aliases = {}
    scratch = []
    if not last:
        out_shape.append(st_shape); out_specs.append(vmem)
        if not first:
            aliases = {len(ins) - 1: n_img}
    else:
        scratch.append(pltpu.VMEM((4, G, SUB, NY) if first else (1, 1, SUB, LANES), jnp.float32))
    pad = pltpu.VMEM((4, G + 2, SUB, NY), jnp.float32)
    scratch += [pad, pad, pad, pltpu.VMEM((2, G, SUB, NY), jnp.float32), pltpu.VMEM((G, SUB, NY), jnp.float32)]
    scratch += [pltpu.SemaphoreType.DMA(())] * 3
    return pl.pallas_call(
        lambda *r: kernel(cfg, *r), out_shape=out_shape, in_specs=in_specs, out_specs=out_specs,
        scratch_shapes=scratch, input_output_aliases=aliases, name=f"depth{'_first' if first else ''}{'_last' if last else ''}",
    )(*ins)


def exchange_path(source, receiver, velocity, anisotropy, omega):
    n = lax.axis_size("freq")
    me = lax.axis_index("freq")
    depth_count, R, NY = velocity.shape
    G = R * n // SUB

    def swap(x, mask):
        return lax.ppermute(x, "freq", [(i, i ^ mask) for i in range(n)])

    blocks = []
    for d in range(depth_count):
        own = jnp.stack([velocity[d], anisotropy[d]])
        mine = jnp.stack([own] + [swap(own, far << 2) for far in range(1, SUB // 2)])
        near = swap(mine, 2)
        blocks.append([mine, near, swap(mine, 1), swap(near, 1)])
    metas = [(0, SUB // 2, False), (SUB // 2, SUB // 2, False), (0, SUB // 2, True), (SUB // 2, SUB // 2, True)]
    where = jnp.stack([me >> 1, me & 1]).astype(jnp.int32)
    states = [(source[p], receiver[p]) for p in range(source.shape[0])]
    layers = []
    for d in range(depth_count):
        total = None
        for p, state in enumerate(states):
            last = d == depth_count - 1
            res = depth_call(where, omega[p : p + 1], blocks[d], metas, state, first=d == 0, last=last, G=G, NY=NY, n_img=2)
            total = res[:2] if total is None else [a + b for a, b in zip(total, res[:2])]
            states[p] = None if last else res[2]
        kept, sent = total
        kept = kept + swap(sent, 1)
        kept = kept[: SUB // 2] + swap(kept[SUB // 2 :], 2)
        image = kept[0]
        for far in range(1, SUB // 2):
            image = image + swap(kept[far], far << 2)
        layers.append(image)
    return jnp.stack(layers)


def gather_path(source, receiver, velocity, anisotropy, omega):
    depth_count = velocity.shape[0]
    both = lax.all_gather(jnp.stack([velocity, anisotropy], axis=1), "freq", axis=2, tiled=True)
    NX, NY = both.shape[2:]
    G = NX // SUB
    order = [((k & 3) << 1) | (k >> 2) for k in range(SUB)]
    back = [order.index(g) for g in range(SUB)]
    both = both.reshape(depth_count, 2, SUB, G, NY)
    both = jnp.stack([both[:, :, g] for g in order], axis=1)
    where = jnp.zeros((2,), jnp.int32)
    states = [(source[p], receiver[p]) for p in range(source.shape[0])]
    layers = []
    for d in range(depth_count):
        total = None
        for p, state in enumerate(states):
            last = d == depth_count - 1
            res = depth_call(where, omega[p : p + 1], [both[d]], [(0, SUB, False)], state, first=d == 0, last=last, G=G, NY=NY, n_img=1)
            total = res[0] if total is None else total + res[0]
            states[p] = None if last else res[1]
        whole = jnp.concatenate([total[k] for k in back], axis=0)
        layers.append(lax.psum_scatter(whole, "freq", scatter_dimension=0, tiled=True))
    return jnp.stack(layers)


def on_device(source, receiver, velocity, anisotropy, frequency):
    pair_count = source.shape[0]
    n = lax.axis_size("freq")
    freq_total = frequency.shape[0]
    pair_ids = lax.axis_index("freq") * pair_count + jnp.arange(pair_count, dtype=jnp.int32)
    lookup = pair_ids[:, None] % freq_total == jnp.arange(freq_total, dtype=jnp.int32)[None, :]
    omega = jnp.sum(jnp.where(lookup, frequency[None, :], 0.0), axis=1)
    exchange = n == 2 * SUB and velocity.shape[1] % SUB == 0
    path = exchange_path if exchange else gather_path
    image = path(source, receiver, velocity, anisotropy, omega)
    return image * (1.0 / math.sqrt(pair_count * n))


def solution(mesh):
    in_specs = (
        P(("survey", "freq"), None, None, None),
        P(("survey", "freq"), None, None, None),
        P("survey", "freq", None),
        P("survey", "freq", None),
        P(),
    )
    out_specs = P("survey", "freq", None)
    return jax.shard_map(
        on_device, mesh=mesh, in_specs=in_specs, out_specs=out_specs, check_vma=False
    )
```

```python
import math
import numpy as np
import jax
import jax.numpy as jnp
from jax import lax
from jax.experimental import pallas as pl
from jax.experimental.pallas import tpu as pltpu
from jax.sharding import PartitionSpec as P


LANES = 128
SUB = 8
UP = 4
U0 = 2
U1 = 8
VLIM = 28 << 20
TOP = 1.7


def even_fit(fun, degree):
    top = TOP * TOP
    nodes = 0.5 * top * (1.0 + np.cos(np.pi * (np.arange(degree + 1) + 0.5) / (degree + 1)))
    return [float(c) for c in np.polynomial.polynomial.polyfit(nodes, fun(np.sqrt(nodes)), degree)]


SIN_C = even_fit(lambda x: np.sin(x) / x, 5)
COS_C = even_fit(np.cos, 6)


def horner(coefs, z):
    acc = z * coefs[-1] + coefs[-2]
    for c in coefs[-3::-1]:
        acc = acc * z + c
    return acc


def off_of(k):
    return ((k & 3) << 1) | (k >> 2)


def at_off(o):
    return ((o & 1) << 2) | (o >> 1)


def cut(b):
    return slice(b * LANES, (b + 1) * LANES)


def iotas():
    return (lax.broadcasted_iota(jnp.int32, (SUB, LANES), 0), lax.broadcasted_iota(jnp.int32, (SUB, LANES), 1))


def pick(parts, which, index):
    out = jnp.take_along_axis(parts[0], index, axis=1)
    for a in range(1, len(parts)):
        out = jnp.where(which == a, jnp.take_along_axis(parts[a], index, axis=1), out)
    return out


def spread(parts):
    nb, lane = len(parts), iotas()[1]
    return [pick(parts, lane // (LANES // nb), (lane * nb + b) % LANES) for b in range(nb)]


def spread4(parts):
    lane = iotas()[1]
    w = LANES // 4
    index = (lane % w) * 4 + lane // w
    p = [jnp.take_along_axis(x, index, axis=1) for x in parts]
    low, even = lane < 2 * w, (lane // w) % 2 == 0
    q = [None] * 4
    for a in range(2):
        x, y = p[a], p[a + 2]
        q[a] = jnp.where(low, x, pltpu.roll(y, 2 * w, 1))
        q[a + 2] = jnp.where(low, pltpu.roll(x, 2 * w, 1), y)
    out = [None] * 4
    for a in (0, 2):
        x, y = q[a], q[a + 1]
        out[a] = jnp.where(even, x, pltpu.roll(y, w, 1))
        out[a + 1] = jnp.where(even, pltpu.roll(x, LANES - w, 1), y)
    return out


def gather_back(parts):
    nb, lane = len(parts), iotas()[1]
    return [pick(parts, lane % nb, lane // nb + a * (LANES // nb)) for a in range(nb)]


def prep_models_kernel(vel, ani, *outs):
    depth, R, NY = vel.shape
    nb = NY // LANES
    for d in range(depth):
        for m, ref in enumerate((vel, ani)):
            for j in range(R // SUB):
                rows = slice(j * SUB, (j + 1) * SUB)
                new = spread([ref[d, rows, cut(b)] for b in range(nb)])
                for b in range(nb):
                    outs[d][m, rows, cut(b)] = new[b]


def prep_models(vel, ani):
    depth, R, NY = vel.shape
    return pl.pallas_call(
        prep_models_kernel, out_shape=[jax.ShapeDtypeStruct((2, R, NY), jnp.float32)] * depth, name="prep_models",
    )(vel, ani)


def prep_fields_kernel(where, src, rcv, out, buf, sem):
    G, NY = out.shape[1], out.shape[3]
    nb = NY // LANES
    chunks = 4
    C = G // chunks
    copies = []
    for h in range(chunks):
        for k in range(SUB):
            row = pl.multiple_of((where[0] ^ off_of(k)) * G + h * C, SUB)
            for a, ref in enumerate((src, rcv)):
                for c in range(2):
                    copies.append(pltpu.make_async_copy(
                        ref.at[c, pl.ds(row, C), :], buf.at[2 * a + c, pl.ds(h * C, C), k, :], sem.at[h]))
    for c in copies:
        c.start()
    for h in range(chunks):
        for c in copies[h * SUB * 4 : (h + 1) * SUB * 4]:
            c.wait()

        def body(j, _):
            for q in range(UP):
                i = j * UP + q
                for a in range(4):
                    new = spread4([buf[a, i, :, cut(b)] for b in range(nb)])
                    for b in range(nb):
                        out[a, i, :, cut(b)] = -new[b] if a == 3 else new[b]
            return 0

        lax.fori_loop(h * C // UP, (h + 1) * C // UP, body, 0)


def prep_fields(where, src, rcv, G, NY):
    shape = (4, G, SUB, NY)
    smem, vmem, anym = (pl.BlockSpec(memory_space=s) for s in (pltpu.SMEM, pltpu.VMEM, pl.ANY))
    return pl.pallas_call(
        prep_fields_kernel, out_shape=jax.ShapeDtypeStruct(shape, jnp.float32), in_specs=[smem, anym, anym], out_specs=vmem,
        scratch_shapes=[pltpu.VMEM(shape, jnp.float32), pltpu.SemaphoreType.DMA((4,))], name="prep_fields",
        compiler_params=pltpu.CompilerParams(vmem_limit_bytes=16 << 20),
    )(where, src, rcv)


def finish_kernel(scale, early, *refs):
    out = refs[-1]
    depth, R, NY = out.shape
    nb = NY // LANES
    for d in range(depth):
        for j in range(R // SUB):
            rows = slice(j * SUB, (j + 1) * SUB)
            parts = []
            for b in range(nb):
                if d < depth - 1:
                    parts.append(early[d, rows, cut(b)] * scale)
                else:
                    v = refs[0][rows, cut(b)]
                    for r in refs[1:-1]:
                        v = v + r[rows, cut(b)]
                    parts.append(v * scale)
            new = gather_back(parts)
            for b in range(nb):
                out[d, rows, cut(b)] = new[b]


def finish(scale, early, tail):
    depth, R, NY = early.shape
    return pl.pallas_call(
        lambda *r: finish_kernel(scale, *r), out_shape=jax.ShapeDtypeStruct((depth + 1, R, NY), jnp.float32), name="finish",
    )(early, *tail)


def wave_tools(where, G, NB):
    me_g = where[0]
    kk, lane = iotas()
    left_edge, right_edge = lane == 0, lane == LANES - 1
    g = me_g ^ off_of(kk)
    up_idx, dn_idx = (at_off(me_g ^ ((g + step) & 7)) for step in (-1, 1))
    has_up, has_dn = g > 0, g < SUB - 1

    def halos(buf):
        for c in range(4):
            for b in range(NB):
                v = buf[c, G, :, cut(b)]
                buf[c, 0, :, cut(b)] = jnp.where(has_up, jnp.take_along_axis(v, up_idx, axis=0), 0.0)
                v = buf[c, 1, :, cut(b)]
                buf[c, G + 1, :, cut(b)] = jnp.where(has_dn, jnp.take_along_axis(v, dn_idx, axis=0), 0.0)

    def around(up, mid, dn):
        r = [a + b for a, b in zip(up, dn)]
        t = [m + 0.25 * a for m, a in zip(mid, r)]
        left = [jnp.where(left_edge, 0.0, pltpu.roll(t[-1], 1, 1))] + t[:-1]
        right = t[1:] + [jnp.where(right_edge, 0.0, pltpu.roll(t[0], LANES - 1, 1))]
        return [a + (b + c) for a, b, c in zip(r, left, right)]

    def sweep(src_buf, put, base, count):
        def body(j, _):
            i0 = base + j * U1
            for f in range(2):
                rows = [[[src_buf[2 * f + c, i0 + q, :, cut(b)] for b in range(NB)] for q in range(U1 + 2)] for c in range(2)]
                for q in range(U1):
                    o = [around(rows[c][q], rows[c][q + 1], rows[c][q + 2]) for c in range(2)]
                    put(f, q, i0 + q, o, [rows[c][q + 1] for c in range(2)])
            return 0

        lax.fori_loop(0, count // U1, body, 0)

    return halos, sweep


def times(mod, i, b, x, y):
    br, bi = mod[0, i, :, cut(b)], mod[1, i, :, cut(b)]
    return br * x - bi * y, br * y + bi * x


def first_kernel(cfg, where, om_ref, *refs):
    metas, R = cfg["metas"], cfg["R"]
    blks, (cur, sh, e1, mod, sem_m) = refs[: len(metas)], refs[len(metas) :]
    G, NB = mod.shape[1], mod.shape[3] // LANES
    lo = where[1]
    bases = [lo * R, (1 - lo) * R][: G // R]
    model_copies = [[] for _ in bases]
    for ref, (k0, kb, half) in zip(blks, metas):
        for k in range(kb):
            for m in range(2):
                model_copies[half].append(pltpu.make_async_copy(
                    ref.at[k, m], mod.at[m, pl.ds(bases[half], R), k0 + k, :], sem_m.at[half]))
    for some in model_copies:
        for c in some:
            c.start()
    halos, sweep = wave_tools(where, G, NB)
    om = om_ref[0]
    k1 = 6.0 / om
    kp = 0.01 * om

    def stage0(i0):
        for q in range(U0):
            i = i0 + q
            for b in range(NB):
                v = mod[0, i, :, cut(b)]
                eta = mod[1, i, :, cut(b)]
                cf = (v * k1) * (1.0 + 2.0 * eta)
                d = cf * (10.0 / 3.0)
                den = 1.0 + d * d
                inv = 1.0 / (v * den)
                ph = kp * (den * inv)
                bi = (cf * (2.0 / 3.0)) * (v * inv)
                mod[0, i, :, cut(b)] = bi * d
                mod[1, i, :, cut(b)] = bi
                z = ph * ph
                sn = ph * horner(SIN_C, z)
                cs = horner(COS_C, z)
                for f in range(2):
                    re, im = cur[2 * f, i, :, cut(b)], cur[2 * f + 1, i, :, cut(b)]
                    sh[2 * f, i + 1, :, cut(b)] = re * cs - im * sn
                    sh[2 * f + 1, i + 1, :, cut(b)] = im * cs + re * sn

    for half, base in enumerate(bases):
        for c in model_copies[half]:
            c.wait()
        lax.fori_loop(0, R // U0, lambda j, _: (stage0(base + j * U0), 0)[1], 0)
    halos(sh)

    def put(f, q, i, o, mid):
        for b in range(NB):
            x, y = times(mod, i, b, o[0][b] - 5.0 * mid[0][b], o[1][b] - 5.0 * mid[1][b])
            e1[2 * f, i + 1, :, cut(b)] = x
            e1[2 * f + 1, i + 1, :, cut(b)] = y

    sweep(sh, put, 0, G)
    halos(e1)


def second_kernel(cfg, where, sh, e1, mod, *refs):
    last, R = cfg["last"], cfg["R"]
    G, NB = mod.shape[1], mod.shape[3] // LANES
    outs, refs = refs[: G // R], list(refs[G // R :])
    lo = where[1]
    bases = [lo * R, (1 - lo) * R][: G // R]
    st, (e2, img, sem_o, *keep) = (None, refs) if last else (refs[0], refs[1:])
    halos, sweep = wave_tools(where, G, NB)

    def put2(f, q, i, o, mid):
        for b in range(NB):
            x, y = times(mod, i, b, o[0][b], o[1][b])
            e2[2 * f, i + 1, :, cut(b)] = x
            e2[2 * f + 1, i + 1, :, cut(b)] = y

    sweep(e1, put2, 0, G)
    halos(e2)

    def put3(f, q, i, o, mid):
        for b in range(NB):
            x, y = times(mod, i, b, o[0][b], o[1][b])
            new = []
            for c, x in enumerate((x, y)):
                total = (x + mid[c][b]) + e1[2 * f + c, i + 1, :, cut(b)]
                new.append(sh[2 * f + c, i + 1, :, cut(b)] + (total + total))
                if not last:
                    st[2 * f + c, i, :, cut(b)] = new[c]
                elif f == 0:
                    keep[0][c, q, :, cut(b)] = new[c]
            if f == 1:
                sr, si = (keep[0][c, q, :, cut(b)] if last else st[c, i, :, cut(b)] for c in range(2))
                img[i, :, cut(b)] = sr * new[0] - si * new[1]

    out_copies = []
    for o_i in reversed(range(len(outs))):
        sweep(e2, put3, bases[o_i], R)
        for k in range(SUB):
            c = pltpu.make_async_copy(img.at[pl.ds(bases[o_i], R), k, :], outs[o_i].at[k], sem_o)
            c.start()
            out_copies.append(c)
    for c in out_copies:
        c.wait()


def spaces():
    return [pl.BlockSpec(memory_space=s) for s in (pltpu.SMEM, pltpu.VMEM, pl.ANY)]


def first_call(where, omega, blocks, metas, state, R):
    _, G, _, NY = state.shape
    smem, vmem, anym = spaces()
    pad = jax.ShapeDtypeStruct((4, G + 2, SUB, NY), jnp.float32)
    return pl.pallas_call(
        lambda *r: first_kernel(dict(metas=metas, R=R), *r), out_shape=[pad, pad, jax.ShapeDtypeStruct((2, G, SUB, NY), jnp.float32)],
        in_specs=[smem, smem] + [anym] * len(blocks) + [vmem], out_specs=[vmem] * 3,
        scratch_shapes=[pltpu.SemaphoreType.DMA((G // R,))], name="first_half",
        compiler_params=pltpu.CompilerParams(vmem_limit_bytes=VLIM),
    )(where, omega, *blocks, state)


def second_call(where, sh, e1, mod, last, R):
    _, G, _, NY = mod.shape
    smem, vmem, anym = spaces()
    out_shape = [jax.ShapeDtypeStruct((SUB, R, NY), jnp.float32)] * (G // R)
    out_specs = [anym] * (G // R)
    if not last:
        out_shape.append(jax.ShapeDtypeStruct((4, G, SUB, NY), jnp.float32))
        out_specs.append(vmem)
    scratch = [pltpu.VMEM((4, G + 2, SUB, NY), jnp.float32), pltpu.VMEM((G, SUB, NY), jnp.float32), pltpu.SemaphoreType.DMA(())]
    if last:
        scratch.append(pltpu.VMEM((2, U1, SUB, NY), jnp.float32))
    return pl.pallas_call(
        lambda *r: second_kernel(dict(last=last, R=R), *r), out_shape=out_shape,
        in_specs=[smem] + [vmem] * 3, out_specs=out_specs,
        scratch_shapes=scratch, name="second_half",
        compiler_params=pltpu.CompilerParams(vmem_limit_bytes=VLIM),
    )(where, sh, e1, mod)


HALF = SUB // 2


def swap(x, mask):
    n = lax.axis_size("freq")
    return lax.ppermute(x, "freq", [(i, i ^ mask) for i in range(n)])


def exchange_path(source, receiver, velocity, anisotropy, omega, scale):
    me = lax.axis_index("freq")
    depth_count, R, NY = velocity.shape
    G = R * lax.axis_size("freq") // SUB
    where = jnp.stack([me >> 1, me & 1]).astype(jnp.int32)
    own = prep_models(velocity, anisotropy)
    states = [prep_fields(where, source[p], receiver[p], G, NY) for p in range(source.shape[0])]
    metas = [(0, HALF, 0), (HALF, HALF, 0), (0, HALF, 1), (HALF, HALF, 1)]
    layers = []
    for d in range(depth_count):
        last = d == depth_count - 1
        parts = [own[d]] + [swap(own[d], far << 2) for far in range(1, HALF)]
        mine = jnp.stack(parts)
        near = swap(mine, 2)
        blocks = [mine, near, swap(mine, 1), swap(near, 1)]
        total = None
        for p, state in enumerate(states):
            mid = first_call(where, omega[p : p + 1], blocks, metas, state, R)
            res = second_call(where, *mid, last, R)
            total = res[:2] if total is None else [a + b for a, b in zip(total, res[:2])]
            states[p] = None if last else res[2]
        kept, sent = total
        got = swap(sent, 1)
        upper = kept[HALF:] + got[HALF:]
        near = swap(upper, 2)
        parts = [(kept[far] + got[far]) + near[far] for far in range(HALF)]
        parts = [parts[0]] + [swap(parts[far], far << 2) for far in range(1, HALF)]
        layers.append(parts if last else sum(parts[1:], parts[0]))
    return finish(scale, jnp.stack(layers[:-1]), layers[-1])


def apart(x):
    nb = x.shape[-1] // LANES
    return jnp.swapaxes(x.reshape(x.shape[:-1] + (LANES, nb)), -1, -2).reshape(x.shape)


def together(x):
    nb = x.shape[-1] // LANES
    return jnp.swapaxes(x.reshape(x.shape[:-1] + (nb, LANES)), -1, -2).reshape(x.shape)


def gather_path(source, receiver, velocity, anisotropy, omega, scale):
    depth_count = velocity.shape[0]
    both = lax.all_gather(apart(jnp.stack([velocity, anisotropy], axis=1)), "freq", axis=2, tiled=True)
    NX, NY = both.shape[2:]
    G = NX // SUB
    places = [off_of(k) for k in range(SUB)]
    back = [places.index(g) for g in range(SUB)]
    both = both.reshape(depth_count, 2, SUB, G, NY)
    both = jnp.stack([both[:, :, g] for g in places], axis=1)
    where = jnp.zeros((2,), jnp.int32)
    states = [prep_fields(where, source[p], receiver[p], G, NY) for p in range(source.shape[0])]
    layers = []
    for d in range(depth_count):
        total = None
        for p, state in enumerate(states):
            last = d == depth_count - 1
            mid = first_call(where, omega[p : p + 1], [both[d]], [(0, SUB, 0)], state, G)
            res = second_call(where, *mid, last, G)
            total = res[0] if total is None else total + res[0]
            states[p] = None if last else res[1]
        whole = jnp.concatenate([total[k] for k in back], axis=0)
        layers.append(lax.psum_scatter(whole, "freq", scatter_dimension=0, tiled=True))
    return together(jnp.stack(layers)) * scale


def use_exchange(n, rows, pairs, depth):
    return n == 2 * SUB and rows % SUB == 0 and pairs == 1 and depth == 4


def on_device(source, receiver, velocity, anisotropy, frequency):
    pair_count = source.shape[0]
    n = lax.axis_size("freq")
    freq_total = frequency.shape[0]
    pair_ids = lax.axis_index("freq") * pair_count + jnp.arange(pair_count, dtype=jnp.int32)
    lookup = pair_ids[:, None] % freq_total == jnp.arange(freq_total, dtype=jnp.int32)[None, :]
    omega = jnp.sum(jnp.where(lookup, frequency[None, :], 0.0), axis=1)
    exchange = use_exchange(n, velocity.shape[1], pair_count, velocity.shape[0])
    path = exchange_path if exchange else gather_path
    return path(source, receiver, velocity, anisotropy, omega, 1.0 / math.sqrt(pair_count * n))


def solution(mesh):
    in_specs = (
        P(("survey", "freq"), None, None, None),
        P(("survey", "freq"), None, None, None),
        P("survey", "freq", None),
        P("survey", "freq", None),
        P(),
    )
    out_specs = P("survey", "freq", None)
    return jax.shard_map(
        on_device, mesh=mesh, in_specs=in_specs, out_specs=out_specs, check_vma=False
    )
```

```python
import math
import numpy as np
import jax
import jax.numpy as jnp
from jax import lax
from jax.experimental import pallas as pl
from jax.experimental.pallas import tpu as pltpu
from jax.sharding import PartitionSpec as P


LANES = 128
SUB = 8
UP = 8
U0 = 2
U1 = 8
VLIM = 28 << 20
TOP = 1.7


def even_fit(fun, degree):
    top = TOP * TOP
    nodes = 0.5 * top * (1.0 + np.cos(np.pi * (np.arange(degree + 1) + 0.5) / (degree + 1)))
    return [float(c) for c in np.polynomial.polynomial.polyfit(nodes, fun(np.sqrt(nodes)), degree)]


SIN_C = even_fit(lambda x: np.sin(x) / x, 5)
COS_C = even_fit(np.cos, 6)


def horner(coefs, z):
    acc = z * coefs[-1] + coefs[-2]
    for c in coefs[-3::-1]:
        acc = acc * z + c
    return acc


def off_of(k):
    return ((k & 3) << 1) | (k >> 2)


def at_off(o):
    return ((o & 1) << 2) | (o >> 1)


def cut(b):
    return slice(b * LANES, (b + 1) * LANES)


def iotas():
    return (lax.broadcasted_iota(jnp.int32, (SUB, LANES), 0), lax.broadcasted_iota(jnp.int32, (SUB, LANES), 1))


def pick(parts, which, index):
    out = jnp.take_along_axis(parts[0], index, axis=1)
    for a in range(1, len(parts)):
        out = jnp.where(which == a, jnp.take_along_axis(parts[a], index, axis=1), out)
    return out


def spread(parts):
    if len(parts) != 4:
        return spread_any(parts)
    lane = iotas()[1]
    w = LANES // 4
    index = (lane % w) * 4 + lane // w
    p = [jnp.take_along_axis(x, index, axis=1) for x in parts]
    low, even = lane < 2 * w, (lane // w) % 2 == 0
    q = [None] * 4
    for a in range(2):
        x, y = p[a], p[a + 2]
        q[a] = jnp.where(low, x, pltpu.roll(y, 2 * w, 1))
        q[a + 2] = jnp.where(low, pltpu.roll(x, 2 * w, 1), y)
    out = [None] * 4
    for a in (0, 2):
        x, y = q[a], q[a + 1]
        out[a] = jnp.where(even, x, pltpu.roll(y, w, 1))
        out[a + 1] = jnp.where(even, pltpu.roll(x, LANES - w, 1), y)
    return out


def spread_any(parts):
    nb, lane = len(parts), iotas()[1]
    return [pick(parts, lane // (LANES // nb), (lane * nb + b) % LANES) for b in range(nb)]


def gather_back(parts):
    nb, lane = len(parts), iotas()[1]
    return [pick(parts, lane % nb, lane // nb + a * (LANES // nb)) for a in range(nb)]


def spaces():
    return [pl.BlockSpec(memory_space=s) for s in (pltpu.SMEM, pltpu.VMEM, pltpu.HBM)]


def prep_models_kernel(depths, vel, ani, *refs):
    outs, (buf, sem) = refs[: len(depths)], refs[len(depths) :]
    _, R, NY = vel.shape
    nb = NY // LANES
    copies = [
        pltpu.make_async_copy(ref.at[d], buf.at[m, n], sem.at[m, n])
        for n, d in enumerate(depths) for m, ref in enumerate((vel, ani))
    ]
    for c in copies:
        c.start()
    for n in range(len(depths)):
        for m in range(2):
            copies[2 * n + m].wait()
            for j in range(R // SUB):
                rows = slice(j * SUB, (j + 1) * SUB)
                new = spread([buf[m, n, rows, cut(b)] for b in range(nb)])
                for b in range(nb):
                    outs[n][m, rows, cut(b)] = new[b]


def prep_models(vel, ani, depths):
    _, R, NY = vel.shape
    _, vmem, hbm = spaces()
    return pl.pallas_call(
        lambda *r: prep_models_kernel(depths, *r), out_shape=[jax.ShapeDtypeStruct((2, R, NY), jnp.float32)] * len(depths),
        in_specs=[hbm, hbm], out_specs=[vmem] * len(depths),
        scratch_shapes=[pltpu.VMEM((2, len(depths), R, NY), jnp.float32), pltpu.SemaphoreType.DMA((2, len(depths)))],
        name="prep_models", compiler_params=pltpu.CompilerParams(vmem_limit_bytes=4 << 20),
    )(vel, ani)


def prep_field_kernel(p, sign, where, field, out, buf, sem):
    G, NY = out.shape[1], out.shape[3]
    nb = NY // LANES
    chunks = sem.shape[0]
    C = G // chunks
    copies = []
    for h in range(chunks):
        for k in range(SUB):
            row = pl.multiple_of((where[0] ^ off_of(k)) * G + h * C, SUB)
            for c in range(2):
                copies.append(pltpu.make_async_copy(
                    field.at[p, c, pl.ds(row, C), :], buf.at[c, pl.ds(h * C, C), k, :], sem.at[h]))
    for c in copies:
        c.start()
    for h in range(chunks):
        for c in copies[h * SUB * 2 : (h + 1) * SUB * 2]:
            c.wait()

        def body(j, _):
            for q in range(UP):
                i = j * UP + q
                for a in range(2):
                    new = spread([buf[a, i, :, cut(b)] for b in range(nb)])
                    for b in range(nb):
                        out[a, i, :, cut(b)] = sign * new[b] if a == 1 and sign < 0 else new[b]
            return 0

        lax.fori_loop(h * C // UP, (h + 1) * C // UP, body, 0)


def prep_field(where, field, p, sign, G):
    NY = field.shape[-1]
    shape = (2, G, SUB, NY)
    smem, vmem, hbm = spaces()
    return pl.pallas_call(
        lambda *r: prep_field_kernel(p, sign, *r), out_shape=jax.ShapeDtypeStruct(shape, jnp.float32), in_specs=[smem, hbm], out_specs=vmem,
        scratch_shapes=[pltpu.VMEM(shape, jnp.float32), pltpu.SemaphoreType.DMA((4,))], name="prep_field",
        compiler_params=pltpu.CompilerParams(vmem_limit_bytes=12 << 20),
    )(where, field)


def finish_early_kernel(scale, early, out, buf, sem):
    depth, R, NY = early.shape
    nb = NY // LANES
    for d in range(depth):
        for j in range(R // SUB):
            rows = slice(j * SUB, (j + 1) * SUB)
            new = gather_back([early[d, rows, cut(b)] * scale for b in range(nb)])
            for b in range(nb):
                buf[d, rows, cut(b)] = new[b]
    copy = pltpu.make_async_copy(buf, out.at[pl.ds(0, depth)], sem)
    copy.start()
    copy.wait()


def finish_early(scale, early):
    depth, R, NY = early.shape
    _, vmem, hbm = spaces()
    return pl.pallas_call(
        lambda *r: finish_early_kernel(scale, *r),
        out_shape=jax.ShapeDtypeStruct((depth + 1, R, NY), jnp.float32), in_specs=[vmem], out_specs=hbm,
        scratch_shapes=[pltpu.VMEM((depth, R, NY), jnp.float32), pltpu.SemaphoreType.DMA(())], name="finish_early",
        compiler_params=pltpu.CompilerParams(vmem_limit_bytes=4 << 20),
    )(early)


def finish_last_kernel(scale, own, *refs):
    far, (before, out, got, buf, sem, sem_o) = refs[:-6], refs[-6:]
    R, NY = buf.shape
    nb = NY // LANES
    copies = [pltpu.make_async_copy(ref, got.at[n], sem.at[n]) for n, ref in enumerate((own, *far))]
    for c in copies:
        c.start()
    for c in copies:
        c.wait()
    for j in range(R // SUB):
        rows = slice(j * SUB, (j + 1) * SUB)
        parts = []
        for b in range(nb):
            v = got[0, rows, cut(b)]
            for n in range(1, got.shape[0]):
                v = v + got[n, rows, cut(b)]
            parts.append(v * scale)
        new = gather_back(parts)
        for b in range(nb):
            buf[rows, cut(b)] = new[b]
    last = pltpu.make_async_copy(buf, out.at[out.shape[0] - 1], sem_o)
    last.start()
    last.wait()


def finish_last(scale, parts, before):
    R, NY = parts[0].shape
    _, _, hbm = spaces()
    n = len(parts)
    return pl.pallas_call(
        lambda *r: finish_last_kernel(scale, *r), out_shape=jax.ShapeDtypeStruct(before.shape, jnp.float32),
        in_specs=[hbm] * (n + 1), out_specs=hbm, input_output_aliases={n: 0},
        scratch_shapes=[pltpu.VMEM((n, R, NY), jnp.float32), pltpu.VMEM((R, NY), jnp.float32), pltpu.SemaphoreType.DMA((n,)), pltpu.SemaphoreType.DMA(())],
        name="finish_last", compiler_params=pltpu.CompilerParams(vmem_limit_bytes=4 << 20),
    )(*parts, before)


def wave_tools(where, G, NB):
    me_g = where[0]
    kk, lane = iotas()
    left_edge, right_edge = lane == 0, lane == LANES - 1
    g = me_g ^ off_of(kk)
    up_idx, dn_idx = (at_off(me_g ^ ((g + step) & 7)) for step in (-1, 1))
    has_up, has_dn = g > 0, g < SUB - 1

    def halos(buf):
        for c in range(4):
            for b in range(NB):
                v = buf[c, G, :, cut(b)]
                buf[c, 0, :, cut(b)] = jnp.where(has_up, jnp.take_along_axis(v, up_idx, axis=0), 0.0)
                v = buf[c, 1, :, cut(b)]
                buf[c, G + 1, :, cut(b)] = jnp.where(has_dn, jnp.take_along_axis(v, dn_idx, axis=0), 0.0)

    def around(up, mid, dn):
        r = [a + b for a, b in zip(up, dn)]
        t = [m + 0.25 * a for m, a in zip(mid, r)]
        left = [jnp.where(left_edge, 0.0, pltpu.roll(t[-1], 1, 1))] + t[:-1]
        right = t[1:] + [jnp.where(right_edge, 0.0, pltpu.roll(t[0], LANES - 1, 1))]
        return [a + (b + c) for a, b, c in zip(r, left, right)]

    def sweep(src_buf, put, base, count):
        def body(j, _):
            i0 = base + j * U1
            for f in range(2):
                rows = [[[src_buf[2 * f + c, i0 + q, :, cut(b)] for b in range(NB)] for q in range(U1 + 2)] for c in range(2)]
                for q in range(U1):
                    o = [around(rows[c][q], rows[c][q + 1], rows[c][q + 2]) for c in range(2)]
                    put(f, q, i0 + q, o, [rows[c][q + 1] for c in range(2)])
            return 0

        lax.fori_loop(0, count // U1, body, 0)

    return halos, sweep


def times(mod, i, b, x, y):
    br, bi = mod[0, i, :, cut(b)], mod[1, i, :, cut(b)]
    return br * x - bi * y, br * y + bi * x


def first_kernel(cfg, where, om_ref, *refs):
    metas, R = cfg["metas"], cfg["R"]
    blks, (*cur, sh, e1, mod, sem_m) = refs[: len(metas)], refs[len(metas) :]
    G, NB = mod.shape[1], mod.shape[3] // LANES
    lo = where[1]
    bases = [lo * R, (1 - lo) * R][: G // R]
    model_copies = [[] for _ in bases]
    for ref, (k0, kb, half) in zip(blks, metas):
        for k in range(kb):
            for m in range(2):
                model_copies[half].append(pltpu.make_async_copy(
                    ref.at[k, m], mod.at[m, pl.ds(bases[half], R), k0 + k, :], sem_m.at[half]))
    for some in model_copies:
        for c in some:
            c.start()
    halos, sweep = wave_tools(where, G, NB)
    om = om_ref[0]
    k1 = 6.0 / om
    kp = 0.01 * om

    def stage0(i0):
        for q in range(U0):
            i = i0 + q
            for b in range(NB):
                v = mod[0, i, :, cut(b)]
                eta = mod[1, i, :, cut(b)]
                cf = (v * k1) * (1.0 + 2.0 * eta)
                d = cf * (10.0 / 3.0)
                den = 1.0 + d * d
                inv = 1.0 / (v * den)
                ph = kp * (den * inv)
                bi = (cf * (2.0 / 3.0)) * (v * inv)
                mod[0, i, :, cut(b)] = bi * d
                mod[1, i, :, cut(b)] = bi
                z = ph * ph
                sn = ph * horner(SIN_C, z)
                cs = horner(COS_C, z)
                for f in range(2):
                    re, im = cur[f][0, i, :, cut(b)], cur[f][1, i, :, cut(b)]
                    sh[2 * f, i + 1, :, cut(b)] = re * cs - im * sn
                    sh[2 * f + 1, i + 1, :, cut(b)] = im * cs + re * sn

    for half, base in enumerate(bases):
        for c in model_copies[half]:
            c.wait()
        lax.fori_loop(0, R // U0, lambda j, _: (stage0(base + j * U0), 0)[1], 0)
    halos(sh)

    def put(f, q, i, o, mid):
        for b in range(NB):
            x, y = times(mod, i, b, o[0][b] - 5.0 * mid[0][b], o[1][b] - 5.0 * mid[1][b])
            e1[2 * f, i + 1, :, cut(b)] = x
            e1[2 * f + 1, i + 1, :, cut(b)] = y

    sweep(sh, put, 0, G)
    halos(e1)


def second_kernel(cfg, where, sh, e1, mod, *refs):
    last, R = cfg["last"], cfg["R"]
    G, NB = mod.shape[1], mod.shape[3] // LANES
    outs, refs = refs[: G // R], list(refs[G // R :])
    lo = where[1]
    bases = [lo * R, (1 - lo) * R][: G // R]
    st, (e2, img, sem_o, *keep) = (None, refs) if last else (refs[:2], refs[2:])
    halos, sweep = wave_tools(where, G, NB)

    def put2(f, q, i, o, mid):
        for b in range(NB):
            x, y = times(mod, i, b, o[0][b], o[1][b])
            e2[2 * f, i + 1, :, cut(b)] = x
            e2[2 * f + 1, i + 1, :, cut(b)] = y

    sweep(e1, put2, 0, G)
    halos(e2)

    def put3(f, q, i, o, mid):
        for b in range(NB):
            x, y = times(mod, i, b, o[0][b], o[1][b])
            new = []
            for c, x in enumerate((x, y)):
                total = (x + mid[c][b]) + e1[2 * f + c, i + 1, :, cut(b)]
                new.append(sh[2 * f + c, i + 1, :, cut(b)] + (total + total))
                if not last:
                    st[f][c, i, :, cut(b)] = new[c]
                elif f == 0:
                    keep[0][c, q, :, cut(b)] = new[c]
            if f == 1:
                sr, si = (keep[0][c, q, :, cut(b)] if last else st[0][c, i, :, cut(b)] for c in range(2))
                img[i, :, cut(b)] = sr * new[0] - si * new[1]

    out_copies = []
    for o_i in reversed(range(len(outs))):
        sweep(e2, put3, bases[o_i], R)
        for k in range(SUB):
            c = pltpu.make_async_copy(img.at[pl.ds(bases[o_i], R), k, :], outs[o_i].at[k], sem_o)
            c.start()
            out_copies.append(c)
    for c in out_copies:
        c.wait()


def first_call(where, omega, blocks, metas, state, R):
    _, G, _, NY = state[0].shape
    smem, vmem, anym = spaces()
    pad = jax.ShapeDtypeStruct((4, G + 2, SUB, NY), jnp.float32)
    return pl.pallas_call(
        lambda *r: first_kernel(dict(metas=metas, R=R), *r), out_shape=[pad, pad, jax.ShapeDtypeStruct((2, G, SUB, NY), jnp.float32)],
        in_specs=[smem, smem] + [anym] * len(blocks) + [vmem] * 2, out_specs=[vmem] * 3,
        scratch_shapes=[pltpu.SemaphoreType.DMA((G // R,))], name="first_half",
        compiler_params=pltpu.CompilerParams(vmem_limit_bytes=VLIM),
    )(where, omega, *blocks, *state)


def second_call(where, sh, e1, mod, last, R):
    _, G, _, NY = mod.shape
    smem, vmem, anym = spaces()
    out_shape = [jax.ShapeDtypeStruct((SUB, R, NY), jnp.float32)] * (G // R)
    out_specs = [anym] * (G // R)
    if not last:
        out_shape += [jax.ShapeDtypeStruct((2, G, SUB, NY), jnp.float32)] * 2
        out_specs += [vmem] * 2
    scratch = [pltpu.VMEM((4, G + 2, SUB, NY), jnp.float32), pltpu.VMEM((G, SUB, NY), jnp.float32), pltpu.SemaphoreType.DMA(())]
    if last:
        scratch.append(pltpu.VMEM((2, U1, SUB, NY), jnp.float32))
    return pl.pallas_call(
        lambda *r: second_kernel(dict(last=last, R=R), *r), out_shape=out_shape,
        in_specs=[smem] + [vmem] * 3, out_specs=out_specs,
        scratch_shapes=scratch, name="second_half",
        compiler_params=pltpu.CompilerParams(vmem_limit_bytes=VLIM),
    )(where, sh, e1, mod)


HALF = SUB // 2


def swap(x, mask):
    n = lax.axis_size("freq")
    return lax.ppermute(x, "freq", [(i, i ^ mask) for i in range(n)])


def exchange_path(source, receiver, velocity, anisotropy, omega, scale):
    me = lax.axis_index("freq")
    depth_count, R, _ = velocity.shape
    G = R * lax.axis_size("freq") // SUB
    where = jnp.stack([me >> 1, me & 1]).astype(jnp.int32)
    own = list(prep_models(velocity, anisotropy, (0,)))
    own += prep_models(velocity, anisotropy, tuple(range(1, depth_count)))
    state = [prep_field(where, source, 0, 1.0, G)]
    state.append(prep_field(where, receiver, 0, -1.0, G))
    metas = [(0, HALF, 0), (HALF, HALF, 0), (0, HALF, 1), (HALF, HALF, 1)]
    early = []
    for d in range(depth_count):
        last = d == depth_count - 1
        parts = [own[d]] + [swap(own[d], far << 2) for far in range(1, HALF)]
        mine = jnp.stack(parts)
        near = swap(mine, 2)
        blocks = [mine, near, swap(mine, 1), swap(near, 1)]
        mid = first_call(where, omega, blocks, metas, state, R)
        kept, sent, *state = second_call(where, *mid, last, R)
        got = swap(sent, 1)
        upper = kept[HALF:] + got[HALF:]
        near = swap(upper, 2)
        if not last:
            early.append((kept, got, near))
        if d == depth_count - 2:
            parts = [jnp.stack([(k[far] + g[far]) + n[far] for k, g, n in early]) for far in range(HALF)]
            parts = [parts[0]] + [swap(parts[far], far << 2) for far in range(1, HALF)]
            before = finish_early(scale, sum(parts[1:], parts[0]))
        if last:
            parts = [(kept[far] + got[far]) + near[far] for far in range(HALF)]
            parts = [parts[0]] + [swap(parts[far], far << 2) for far in range(1, HALF)]
            return finish_last(scale, parts, before)


def apart(x):
    nb = x.shape[-1] // LANES
    return jnp.swapaxes(x.reshape(x.shape[:-1] + (LANES, nb)), -1, -2).reshape(x.shape)


def together(x):
    nb = x.shape[-1] // LANES
    return jnp.swapaxes(x.reshape(x.shape[:-1] + (nb, LANES)), -1, -2).reshape(x.shape)


def gather_path(source, receiver, velocity, anisotropy, omega, scale):
    depth_count = velocity.shape[0]
    both = lax.all_gather(apart(jnp.stack([velocity, anisotropy], axis=1)), "freq", axis=2, tiled=True)
    NX, NY = both.shape[2:]
    G = NX // SUB
    places = [off_of(k) for k in range(SUB)]
    back = [places.index(g) for g in range(SUB)]
    both = both.reshape(depth_count, 2, SUB, G, NY)
    both = jnp.stack([both[:, :, g] for g in places], axis=1)
    where = jnp.zeros((2,), jnp.int32)
    states = [[prep_field(where, source, p, 1.0, G), prep_field(where, receiver, p, -1.0, G)] for p in range(source.shape[0])]
    layers = []
    for d in range(depth_count):
        total = None
        for p, state in enumerate(states):
            last = d == depth_count - 1
            mid = first_call(where, omega[p : p + 1], [both[d]], [(0, SUB, 0)], state, G)
            res = second_call(where, *mid, last, G)
            total = res[0] if total is None else total + res[0]
            states[p] = None if last else res[1:]
        whole = jnp.concatenate([total[k] for k in back], axis=0)
        layers.append(lax.psum_scatter(whole, "freq", scatter_dimension=0, tiled=True))
    return together(jnp.stack(layers)) * scale


def use_exchange(n, rows, pairs, depth):
    return n == 2 * SUB and rows % SUB == 0 and pairs == 1 and depth == 4


def on_device(source, receiver, velocity, anisotropy, frequency):
    pair_count = source.shape[0]
    n = lax.axis_size("freq")
    freq_total = frequency.shape[0]
    pair_ids = lax.axis_index("freq") * pair_count + jnp.arange(pair_count, dtype=jnp.int32)
    lookup = pair_ids[:, None] % freq_total == jnp.arange(freq_total, dtype=jnp.int32)[None, :]
    omega = jnp.sum(jnp.where(lookup, frequency[None, :], 0.0), axis=1)
    exchange = use_exchange(n, velocity.shape[1], pair_count, velocity.shape[0])
    path = exchange_path if exchange else gather_path
    return path(source, receiver, velocity, anisotropy, omega, 1.0 / math.sqrt(pair_count * n))


def solution(mesh):
    in_specs = (
        P(("survey", "freq"), None, None, None),
        P(("survey", "freq"), None, None, None),
        P("survey", "freq", None),
        P("survey", "freq", None),
        P(),
    )
    out_specs = P("survey", "freq", None)
    return jax.shard_map(
        on_device, mesh=mesh, in_specs=in_specs, out_specs=out_specs, check_vma=False
    )
```

```python
import math
import numpy as np
import jax
import jax.numpy as jnp
from jax import lax
from jax.experimental import pallas as pl
from jax.experimental.pallas import tpu as pltpu
from jax.sharding import PartitionSpec as P


LANES = 128
SUB = 8
U1 = SUB
VLIM = 28 << 20
TOP = 1.7


def even_fit(fun, degree):
    top = TOP * TOP
    nodes = 0.5 * top * (1.0 + np.cos(np.pi * (np.arange(degree + 1) + 0.5) / (degree + 1)))
    return [float(c) for c in np.polynomial.polynomial.polyfit(nodes, fun(np.sqrt(nodes)), degree)]


SIN_C = even_fit(lambda x: np.sin(x) / x, 4)
COS_C = even_fit(np.cos, 5)


def horner(coefs, z):
    acc = z * coefs[-1] + coefs[-2]
    for c in coefs[-3::-1]:
        acc = acc * z + c
    return acc


def off_of(k):
    return ((k & 3) << 1) | (k >> 2)


def at_off(o):
    return ((o & 1) << 2) | (o >> 1)


def cut(b):
    return slice(b * LANES, (b + 1) * LANES)


def iotas():
    return (lax.broadcasted_iota(jnp.int32, (SUB, LANES), 0), lax.broadcasted_iota(jnp.int32, (SUB, LANES), 1))


def pick(parts, which, index):
    out = jnp.take_along_axis(parts[0], index, axis=1)
    for a in range(1, len(parts)):
        out = jnp.where(which == a, jnp.take_along_axis(parts[a], index, axis=1), out)
    return out


def spread(parts):
    if len(parts) != 4:
        return spread_any(parts)
    lane = iotas()[1]
    w = LANES // 4
    index = (lane % w) * 4 + lane // w
    p = [jnp.take_along_axis(x, index, axis=1) for x in parts]
    low, even = lane < 2 * w, (lane // w) % 2 == 0
    q = [None] * 4
    for a in range(2):
        x, y = p[a], p[a + 2]
        q[a] = jnp.where(low, x, pltpu.roll(y, 2 * w, 1))
        q[a + 2] = jnp.where(low, pltpu.roll(x, 2 * w, 1), y)
    out = [None] * 4
    for a in (0, 2):
        x, y = q[a], q[a + 1]
        out[a] = jnp.where(even, x, pltpu.roll(y, w, 1))
        out[a + 1] = jnp.where(even, pltpu.roll(x, LANES - w, 1), y)
    return out


def turn(v):
    sub = iotas()[0]
    v = list(v)
    step = SUB // 2
    while step:
        low = (sub & step) == 0
        for a in range(SUB):
            if a & step == 0:
                x, y = v[a], v[a + step]
                v[a] = jnp.where(low, x, pltpu.roll(y, step, 0))
                v[a + step] = jnp.where(low, pltpu.roll(x, SUB - step, 0), y)
        step //= 2
    return v


def spread_any(parts):
    nb, lane = len(parts), iotas()[1]
    return [pick(parts, lane // (LANES // nb), (lane * nb + b) % LANES) for b in range(nb)]


def gather_back(parts):
    nb, lane = len(parts), iotas()[1]
    return [pick(parts, lane % nb, lane // nb + a * (LANES // nb)) for a in range(nb)]


def spaces():
    return [pl.BlockSpec(memory_space=s) for s in (pltpu.SMEM, pltpu.VMEM, pltpu.HBM)]


def prep_models_kernel(depths, vel, ani, *outs):
    _, R, NY = vel.shape
    nb = NY // LANES
    for n, d in enumerate(depths):
        for m, ref in enumerate((vel, ani)):
            for j in range(R // SUB):
                rows = slice(j * SUB, (j + 1) * SUB)
                new = spread([ref[d, rows, cut(b)] for b in range(nb)])
                for b in range(nb):
                    outs[n][m, rows, cut(b)] = new[b]


def prep_models(vel, ani, depths):
    _, R, NY = vel.shape
    _, vmem, _ = spaces()
    return pl.pallas_call(
        lambda *r: prep_models_kernel(depths, *r), out_shape=[jax.ShapeDtypeStruct((2, R, NY), jnp.float32)] * len(depths),
        in_specs=[vmem] * 2, out_specs=[vmem] * len(depths),
        name="prep_models", compiler_params=pltpu.CompilerParams(vmem_limit_bytes=4 << 20),
    )(vel, ani)


def prep_field_kernel(p, sign, where, field, out):
    G, NY = out.shape[1], out.shape[3]
    nb = NY // LANES
    starts = [(where[0] ^ off_of(k)) * G for k in range(SUB)]

    def body(j, _):
        for c in range(2):
            cols = []
            for b in range(nb):
                rows = [field[p, c, pl.ds(pl.multiple_of(starts[k] + j * SUB, SUB), SUB), cut(b)] for k in range(SUB)]
                cols.append(turn(rows))
            for q in range(SUB):
                new = spread([cols[b][q] for b in range(nb)])
                for b in range(nb):
                    out[c, j * SUB + q, :, cut(b)] = -new[b] if c == 1 and sign < 0 else new[b]
        return 0

    lax.fori_loop(0, G // SUB, body, 0)


def prep_field(where, field, p, sign, G):
    NY = field.shape[-1]
    shape = (2, G, SUB, NY)
    smem, vmem, _ = spaces()
    return pl.pallas_call(
        lambda *r: prep_field_kernel(p, sign, *r), out_shape=jax.ShapeDtypeStruct(shape, jnp.float32), in_specs=[smem, vmem], out_specs=vmem, name="prep_field",
        compiler_params=pltpu.CompilerParams(vmem_limit_bytes=12 << 20),
    )(where, field)


def finish_early_kernel(scale, early, out, buf, sem):
    depth, R, NY = early.shape
    nb = NY // LANES
    for d in range(depth):
        for j in range(R // SUB):
            rows = slice(j * SUB, (j + 1) * SUB)
            new = gather_back([early[d, rows, cut(b)] * scale for b in range(nb)])
            for b in range(nb):
                buf[d, rows, cut(b)] = new[b]
    copy = pltpu.make_async_copy(buf, out.at[pl.ds(0, depth)], sem)
    copy.start()
    copy.wait()


def finish_early(scale, early):
    depth, R, NY = early.shape
    _, vmem, hbm = spaces()
    return pl.pallas_call(
        lambda *r: finish_early_kernel(scale, *r),
        out_shape=jax.ShapeDtypeStruct((depth + 1, R, NY), jnp.float32), in_specs=[vmem], out_specs=hbm,
        scratch_shapes=[pltpu.VMEM((depth, R, NY), jnp.float32), pltpu.SemaphoreType.DMA(())], name="finish_early",
        compiler_params=pltpu.CompilerParams(vmem_limit_bytes=4 << 20),
    )(early)


def finish_last_kernel(scale, own, *refs):
    far, (before, out, got, buf, sem, sem_o) = refs[:-6], refs[-6:]
    R, NY = buf.shape
    nb = NY // LANES
    copies = [pltpu.make_async_copy(ref, got.at[n], sem.at[n]) for n, ref in enumerate((own, *far))]
    for c in copies:
        c.start()
    for c in copies:
        c.wait()
    for j in range(R // SUB):
        rows = slice(j * SUB, (j + 1) * SUB)
        parts = []
        for b in range(nb):
            v = got[0, rows, cut(b)]
            for n in range(1, got.shape[0]):
                v = v + got[n, rows, cut(b)]
            parts.append(v * scale)
        new = gather_back(parts)
        for b in range(nb):
            buf[rows, cut(b)] = new[b]
    last = pltpu.make_async_copy(buf, out.at[out.shape[0] - 1], sem_o)
    last.start()
    last.wait()


def finish_last(scale, parts, before):
    R, NY = parts[0].shape
    _, _, hbm = spaces()
    n = len(parts)
    return pl.pallas_call(
        lambda *r: finish_last_kernel(scale, *r), out_shape=jax.ShapeDtypeStruct(before.shape, jnp.float32),
        in_specs=[hbm] * (n + 1), out_specs=hbm, input_output_aliases={n: 0},
        scratch_shapes=[pltpu.VMEM((n, R, NY), jnp.float32), pltpu.VMEM((R, NY), jnp.float32), pltpu.SemaphoreType.DMA((n,)), pltpu.SemaphoreType.DMA(())],
        name="finish_last", compiler_params=pltpu.CompilerParams(vmem_limit_bytes=4 << 20),
    )(*parts, before)


def wave_tools(where, G, NB):
    me_g = where[0]
    kk, lane = iotas()
    left_edge, right_edge = lane == 0, lane == LANES - 1
    g = me_g ^ off_of(kk)
    up_idx, dn_idx = (at_off(me_g ^ ((g + step) & 7)) for step in (-1, 1))
    has_up, has_dn = g > 0, g < SUB - 1

    def halos(buf):
        for c in range(4):
            for b in range(NB):
                v = buf[c, G, :, cut(b)]
                buf[c, 0, :, cut(b)] = jnp.where(has_up, jnp.take_along_axis(v, up_idx, axis=0), 0.0)
                v = buf[c, 1, :, cut(b)]
                buf[c, G + 1, :, cut(b)] = jnp.where(has_dn, jnp.take_along_axis(v, dn_idx, axis=0), 0.0)

    def around(up, mid, dn):
        r = [a + b for a, b in zip(up, dn)]
        t = [m + 0.25 * a for m, a in zip(mid, r)]
        left = [jnp.where(left_edge, 0.0, pltpu.roll(t[-1], 1, 1))] + t[:-1]
        right = t[1:] + [jnp.where(right_edge, 0.0, pltpu.roll(t[0], LANES - 1, 1))]
        return [a + (b + c) for a, b, c in zip(r, left, right)]

    def sweep(src_buf, put, base, count, done=None):
        def body(j, _):
            i0 = base + j * U1
            for f in range(2):
                rows = [[[src_buf[2 * f + c, i0 + q, :, cut(b)] for b in range(NB)] for q in range(U1 + 2)] for c in range(2)]
                for q in range(U1):
                    o = [around(rows[c][q], rows[c][q + 1], rows[c][q + 2]) for c in range(2)]
                    put(f, q, i0 + q, o, [rows[c][q + 1] for c in range(2)])
            if done is not None:
                done(i0)
            return 0

        lax.fori_loop(0, count // U1, body, 0)

    return halos, sweep


def times(mod, i, b, x, y):
    br, bi = mod[0, i, :, cut(b)], mod[1, i, :, cut(b)]
    return br * x - bi * y, br * y + bi * x


def first_kernel(cfg, where, om_ref, *refs):
    metas, R = cfg["metas"], cfg["R"]
    blks, (*cur, sh, e1, mod) = refs[: len(metas)], refs[len(metas) :]
    G, NB = mod.shape[1], mod.shape[3] // LANES
    lo = where[1]
    bases = [lo * R, (1 - lo) * R][: G // R]
    places = [[None] * SUB for _ in bases]
    for ref, (k0, kb, half) in zip(blks, metas):
        for k in range(kb):
            places[half][k0 + k] = (ref, k)
    halos, sweep = wave_tools(where, G, NB)
    om = om_ref[0]
    k1 = 6.0 / om
    kp = 0.01 * om

    def cell(i, b, v, eta):
        cf = (v * k1) * (1.0 + 2.0 * eta)
        d = cf * (10.0 / 3.0)
        den = 1.0 + d * d
        inv = 1.0 / (v * den)
        ph = kp * (den * inv)
        bi = (cf * (2.0 / 3.0)) * (v * inv)
        mod[0, i, :, cut(b)] = bi * d
        mod[1, i, :, cut(b)] = bi
        z = ph * ph
        sn = ph * horner(SIN_C, z)
        cs = horner(COS_C, z)
        for f in range(2):
            re, im = cur[f][0, i, :, cut(b)], cur[f][1, i, :, cut(b)]
            sh[2 * f, i + 1, :, cut(b)] = re * cs - im * sn
            sh[2 * f + 1, i + 1, :, cut(b)] = im * cs + re * sn

    for half, base in enumerate(bases):
        def stage0(j, _):
            rows = pl.ds(pl.multiple_of(j * SUB, SUB), SUB)
            for b in range(NB):
                v, eta = (turn([ref[k, m, rows, cut(b)] for ref, k in places[half]]) for m in range(2))
                for q in range(SUB):
                    cell(base + j * SUB + q, b, v[q], eta[q])
            return 0

        lax.fori_loop(0, R // SUB, stage0, 0)
    halos(sh)

    def put(f, q, i, o, mid):
        for b in range(NB):
            x, y = times(mod, i, b, o[0][b] - 5.0 * mid[0][b], o[1][b] - 5.0 * mid[1][b])
            e1[2 * f, i + 1, :, cut(b)] = x
            e1[2 * f + 1, i + 1, :, cut(b)] = y

    sweep(sh, put, 0, G)
    halos(e1)


def second_kernel(cfg, where, sh, e1, mod, *refs):
    last, R = cfg["last"], cfg["R"]
    G, NB = mod.shape[1], mod.shape[3] // LANES
    outs, refs = refs[: G // R], list(refs[G // R :])
    lo = where[1]
    bases = [lo * R, (1 - lo) * R][: G // R]
    st, (e2, *keep) = (None, refs) if last else (refs[:2], refs[2:])
    halos, sweep = wave_tools(where, G, NB)

    def put2(f, q, i, o, mid):
        for b in range(NB):
            x, y = times(mod, i, b, o[0][b], o[1][b])
            e2[2 * f, i + 1, :, cut(b)] = x
            e2[2 * f + 1, i + 1, :, cut(b)] = y

    sweep(e1, put2, 0, G)
    halos(e2)

    def put3(f, q, i, o, mid):
        for b in range(NB):
            x, y = times(mod, i, b, o[0][b], o[1][b])
            new = []
            for c, x in enumerate((x, y)):
                total = (x + mid[c][b]) + e1[2 * f + c, i + 1, :, cut(b)]
                new.append(sh[2 * f + c, i + 1, :, cut(b)] + (total + total))
                if not last:
                    st[f][c, i, :, cut(b)] = new[c]
                elif f == 0:
                    keep[0][c, q, :, cut(b)] = new[c]
            if f == 1:
                sr, si = (keep[0][c, q, :, cut(b)] if last else st[0][c, i, :, cut(b)] for c in range(2))
                images[b][q] = sr * new[0] - si * new[1]

    images = [[None] * SUB for _ in range(NB)]
    for o_i in reversed(range(len(outs))):
        def send(i0):
            rows = pl.ds(pl.multiple_of(i0 - bases[o_i], SUB), SUB)
            for b in range(NB):
                for k, v in enumerate(turn(images[b])):
                    outs[o_i][k, rows, cut(b)] = v

        sweep(e2, put3, bases[o_i], R, send)


def first_call(where, omega, blocks, metas, state, R):
    _, G, _, NY = state[0].shape
    smem, vmem, _ = spaces()
    pad = jax.ShapeDtypeStruct((4, G + 2, SUB, NY), jnp.float32)
    return pl.pallas_call(
        lambda *r: first_kernel(dict(metas=metas, R=R), *r), out_shape=[pad, pad, jax.ShapeDtypeStruct((2, G, SUB, NY), jnp.float32)],
        in_specs=[smem, smem] + [vmem] * (len(blocks) + 2), out_specs=[vmem] * 3, name="first_half",
        compiler_params=pltpu.CompilerParams(vmem_limit_bytes=VLIM),
    )(where, omega, *blocks, *state)


def second_call(where, sh, e1, mod, last, R):
    _, G, _, NY = mod.shape
    smem, vmem, _ = spaces()
    out_shape = [jax.ShapeDtypeStruct((SUB, R, NY), jnp.float32)] * (G // R)
    out_specs = [vmem] * (G // R)
    if not last:
        out_shape += [jax.ShapeDtypeStruct((2, G, SUB, NY), jnp.float32)] * 2
        out_specs += [vmem] * 2
    scratch = [pltpu.VMEM((4, G + 2, SUB, NY), jnp.float32)]
    if last:
        scratch.append(pltpu.VMEM((2, U1, SUB, NY), jnp.float32))
    return pl.pallas_call(
        lambda *r: second_kernel(dict(last=last, R=R), *r), out_shape=out_shape,
        in_specs=[smem] + [vmem] * 3, out_specs=out_specs,
        scratch_shapes=scratch, name="second_half",
        compiler_params=pltpu.CompilerParams(vmem_limit_bytes=VLIM),
    )(where, sh, e1, mod)


HALF = SUB // 2


def swap(x, mask):
    n = lax.axis_size("freq")
    return lax.ppermute(x, "freq", [(i, i ^ mask) for i in range(n)])


def exchange_path(source, receiver, velocity, anisotropy, omega, scale):
    me = lax.axis_index("freq")
    depth_count, R, _ = velocity.shape
    G = R * lax.axis_size("freq") // SUB
    where = jnp.stack([me >> 1, me & 1]).astype(jnp.int32)
    own = list(prep_models(velocity, anisotropy, (0,)))
    own += prep_models(velocity, anisotropy, tuple(range(1, depth_count)))
    state = [prep_field(where, source, 0, 1.0, G)]
    state.append(prep_field(where, receiver, 0, -1.0, G))
    metas = [(0, HALF, 0), (HALF, HALF, 0), (0, HALF, 1), (HALF, HALF, 1)]
    early = []
    for d in range(depth_count):
        last = d == depth_count - 1
        parts = [own[d]] + [swap(own[d], far << 2) for far in range(1, HALF)]
        mine = jnp.stack(parts)
        near = swap(mine, 2)
        blocks = [mine, near, swap(mine, 1), swap(near, 1)]
        mid = first_call(where, omega, blocks, metas, state, R)
        kept, sent, *state = second_call(where, *mid, last, R)
        got = swap(sent, 1)
        upper = kept[HALF:] + got[HALF:]
        near = swap(upper, 2)
        if not last:
            early.append((kept, got, near))
        if d == depth_count - 2:
            parts = [jnp.stack([(k[far] + g[far]) + n[far] for k, g, n in early]) for far in range(HALF)]
            parts = [parts[0]] + [swap(parts[far], far << 2) for far in range(1, HALF)]
            before = finish_early(scale, sum(parts[1:], parts[0]))
        if last:
            parts = [(kept[far] + got[far]) + near[far] for far in range(HALF)]
            parts = [parts[0]] + [swap(parts[far], far << 2) for far in range(1, HALF)]
            return finish_last(scale, parts, before)


def apart(x):
    nb = x.shape[-1] // LANES
    return jnp.swapaxes(x.reshape(x.shape[:-1] + (LANES, nb)), -1, -2).reshape(x.shape)


def together(x):
    nb = x.shape[-1] // LANES
    return jnp.swapaxes(x.reshape(x.shape[:-1] + (nb, LANES)), -1, -2).reshape(x.shape)


def gather_path(source, receiver, velocity, anisotropy, omega, scale):
    depth_count = velocity.shape[0]
    both = lax.all_gather(apart(jnp.stack([velocity, anisotropy], axis=1)), "freq", axis=2, tiled=True)
    NX, NY = both.shape[2:]
    G = NX // SUB
    places = [off_of(k) for k in range(SUB)]
    back = [places.index(g) for g in range(SUB)]
    both = both.reshape(depth_count, 2, SUB, G, NY)
    both = jnp.stack([both[:, :, g] for g in places], axis=1)
    where = jnp.zeros((2,), jnp.int32)
    states = [[prep_field(where, source, p, 1.0, G), prep_field(where, receiver, p, -1.0, G)] for p in range(source.shape[0])]
    layers = []
    for d in range(depth_count):
        total = None
        for p, state in enumerate(states):
            last = d == depth_count - 1
            mid = first_call(where, omega[p : p + 1], [both[d]], [(0, SUB, 0)], state, G)
            res = second_call(where, *mid, last, G)
            total = res[0] if total is None else total + res[0]
            states[p] = None if last else res[1:]
        whole = jnp.concatenate([total[k] for k in back], axis=0)
        layers.append(lax.psum_scatter(whole, "freq", scatter_dimension=0, tiled=True))
    return together(jnp.stack(layers)) * scale


def use_exchange(n, rows, pairs, depth):
    return n == 2 * SUB and rows % SUB == 0 and pairs == 1 and depth == 4


def on_device(source, receiver, velocity, anisotropy, frequency):
    pair_count = source.shape[0]
    n = lax.axis_size("freq")
    freq_total = frequency.shape[0]
    pair_ids = lax.axis_index("freq") * pair_count + jnp.arange(pair_count, dtype=jnp.int32)
    lookup = pair_ids[:, None] % freq_total == jnp.arange(freq_total, dtype=jnp.int32)[None, :]
    omega = jnp.sum(jnp.where(lookup, frequency[None, :], 0.0), axis=1)
    exchange = use_exchange(n, velocity.shape[1], pair_count, velocity.shape[0])
    path = exchange_path if exchange else gather_path
    return path(source, receiver, velocity, anisotropy, omega, 1.0 / math.sqrt(pair_count * n))


def solution(mesh):
    in_specs = (
        P(("survey", "freq"), None, None, None),
        P(("survey", "freq"), None, None, None),
        P("survey", "freq", None),
        P("survey", "freq", None),
        P(),
    )
    out_specs = P("survey", "freq", None)
    return jax.shard_map(
        on_device, mesh=mesh, in_specs=in_specs, out_specs=out_specs, check_vma=False
    )
```

```python
import math
import numpy as np
import jax
import jax.numpy as jnp
from jax import lax
from jax.experimental import pallas as pl
from jax.experimental.pallas import tpu as pltpu
from jax.sharding import PartitionSpec as P


LANES = 128
SUB = 8
U1 = SUB
VLIM = 28 << 20
TOP = 1.7


def even_fit(fun, degree):
    top = TOP * TOP
    nodes = 0.5 * top * (1.0 + np.cos(np.pi * (np.arange(degree + 1) + 0.5) / (degree + 1)))
    return [float(c) for c in np.polynomial.polynomial.polyfit(nodes, fun(np.sqrt(nodes)), degree)]


SIN_C = even_fit(lambda x: np.sin(x) / x, 4)
COS_C = even_fit(np.cos, 5)


def horner(coefs, z):
    acc = z * coefs[-1] + coefs[-2]
    for c in coefs[-3::-1]:
        acc = acc * z + c
    return acc


def off_of(k):
    return ((k & 3) << 1) | (k >> 2)


def at_off(o):
    return ((o & 1) << 2) | (o >> 1)


def cut(b):
    return slice(b * LANES, (b + 1) * LANES)


def iotas():
    return (lax.broadcasted_iota(jnp.int32, (SUB, LANES), 0), lax.broadcasted_iota(jnp.int32, (SUB, LANES), 1))


def pick(parts, which, index):
    out = jnp.take_along_axis(parts[0], index, axis=1)
    for a in range(1, len(parts)):
        out = jnp.where(which == a, jnp.take_along_axis(parts[a], index, axis=1), out)
    return out


def spread(parts):
    if len(parts) != 4:
        return spread_any(parts)
    lane = iotas()[1]
    w = LANES // 4
    index = (lane % w) * 4 + lane // w
    p = [jnp.take_along_axis(x, index, axis=1) for x in parts]
    low, even = lane < 2 * w, (lane // w) % 2 == 0
    q = [None] * 4
    for a in range(2):
        x, y = p[a], p[a + 2]
        q[a] = jnp.where(low, x, pltpu.roll(y, 2 * w, 1))
        q[a + 2] = jnp.where(low, pltpu.roll(x, 2 * w, 1), y)
    out = [None] * 4
    for a in (0, 2):
        x, y = q[a], q[a + 1]
        out[a] = jnp.where(even, x, pltpu.roll(y, w, 1))
        out[a + 1] = jnp.where(even, pltpu.roll(x, LANES - w, 1), y)
    return out


def turn(v):
    sub = iotas()[0]
    v = list(v)
    step = SUB // 2
    while step:
        low = (sub & step) == 0
        for a in range(SUB):
            if a & step == 0:
                x, y = v[a], v[a + step]
                v[a] = jnp.where(low, x, pltpu.roll(y, step, 0))
                v[a + step] = jnp.where(low, pltpu.roll(x, SUB - step, 0), y)
        step //= 2
    return v


def spread_any(parts):
    nb, lane = len(parts), iotas()[1]
    return [pick(parts, lane // (LANES // nb), (lane * nb + b) % LANES) for b in range(nb)]


def gather_back(parts):
    nb, lane = len(parts), iotas()[1]
    return [pick(parts, lane % nb, lane // nb + a * (LANES // nb)) for a in range(nb)]


def spaces():
    return [pl.BlockSpec(memory_space=s) for s in (pltpu.SMEM, pltpu.VMEM, pltpu.HBM)]


def prep_models_kernel(depths, vel, ani, *outs):
    _, R, NY = vel.shape
    nb = NY // LANES
    for d in range(vel.shape[0]) if len(outs) > len(depths) else depths:
        for m, ref in enumerate((vel, ani)):
            for j in range(R // SUB):
                rows = slice(j * SUB, (j + 1) * SUB)
                new = spread([ref[d, rows, cut(b)] for b in range(nb)])
                for b in range(nb):
                    if d in depths:
                        outs[depths.index(d)][m, rows, cut(b)] = new[b]
                    if len(outs) > len(depths):
                        outs[-1][d, m, rows, cut(b)] = new[b]


def prep_models(vel, ani, depths, everything):
    depth, R, NY = vel.shape
    _, vmem, _ = spaces()
    shapes = [(2, R, NY)] * len(depths) + [(depth, 2, R, NY)] * everything
    return pl.pallas_call(
        lambda *r: prep_models_kernel(depths, *r), out_shape=[jax.ShapeDtypeStruct(x, jnp.float32) for x in shapes],
        in_specs=[vmem] * 2, out_specs=[vmem] * len(shapes),
        name="prep_models", compiler_params=pltpu.CompilerParams(vmem_limit_bytes=4 << 20),
    )(vel, ani)


def prep_field_kernel(p, sign, where, field, out):
    G, NY = out.shape[1], out.shape[3]
    nb = NY // LANES
    starts = [(where[0] ^ off_of(k)) * G for k in range(SUB)]

    def body(j, _):
        for c in range(2):
            cols = []
            for b in range(nb):
                rows = [field[p, c, pl.ds(pl.multiple_of(starts[k] + j * SUB, SUB), SUB), cut(b)] for k in range(SUB)]
                cols.append(turn(rows))
            for q in range(SUB):
                new = spread([cols[b][q] for b in range(nb)])
                for b in range(nb):
                    out[c, j * SUB + q, :, cut(b)] = -new[b] if c == 1 and sign < 0 else new[b]
        return 0

    lax.fori_loop(0, G // SUB, body, 0)


def prep_field(where, field, p, sign, G):
    NY = field.shape[-1]
    shape = (2, G, SUB, NY)
    smem, vmem, _ = spaces()
    return pl.pallas_call(
        lambda *r: prep_field_kernel(p, sign, *r), out_shape=jax.ShapeDtypeStruct(shape, jnp.float32), in_specs=[smem, vmem], out_specs=vmem, name="prep_field",
        compiler_params=pltpu.CompilerParams(vmem_limit_bytes=12 << 20),
    )(where, field)


def finish_early_kernel(scale, early, out, buf, sem):
    depth, R, NY = early.shape
    nb = NY // LANES
    for d in range(depth):
        for j in range(R // SUB):
            rows = slice(j * SUB, (j + 1) * SUB)
            new = gather_back([early[d, rows, cut(b)] * scale for b in range(nb)])
            for b in range(nb):
                buf[d, rows, cut(b)] = new[b]
    copy = pltpu.make_async_copy(buf, out.at[pl.ds(0, depth)], sem)
    copy.start()
    copy.wait()


def finish_early(scale, early):
    depth, R, NY = early.shape
    _, vmem, hbm = spaces()
    return pl.pallas_call(
        lambda *r: finish_early_kernel(scale, *r),
        out_shape=jax.ShapeDtypeStruct((depth + 1, R, NY), jnp.float32), in_specs=[vmem], out_specs=hbm,
        scratch_shapes=[pltpu.VMEM((depth, R, NY), jnp.float32), pltpu.SemaphoreType.DMA(())], name="finish_early",
        compiler_params=pltpu.CompilerParams(vmem_limit_bytes=4 << 20),
    )(early)


def finish_last_kernel(scale, own, *refs):
    far, (before, out, got, buf, sem, sem_o) = refs[:-6], refs[-6:]
    R, NY = buf.shape
    nb = NY // LANES
    copies = [pltpu.make_async_copy(ref, got.at[n], sem.at[n]) for n, ref in enumerate((own, *far))]
    for c in copies:
        c.start()
    for c in copies:
        c.wait()
    for j in range(R // SUB):
        rows = slice(j * SUB, (j + 1) * SUB)
        parts = []
        for b in range(nb):
            v = got[0, rows, cut(b)]
            for n in range(1, got.shape[0]):
                v = v + got[n, rows, cut(b)]
            parts.append(v * scale)
        new = gather_back(parts)
        for b in range(nb):
            buf[rows, cut(b)] = new[b]
    last = pltpu.make_async_copy(buf, out.at[out.shape[0] - 1], sem_o)
    last.start()
    last.wait()


def finish_last(scale, parts, before):
    R, NY = parts[0].shape
    _, _, hbm = spaces()
    n = len(parts)
    return pl.pallas_call(
        lambda *r: finish_last_kernel(scale, *r), out_shape=jax.ShapeDtypeStruct(before.shape, jnp.float32),
        in_specs=[hbm] * (n + 1), out_specs=hbm, input_output_aliases={n: 0},
        scratch_shapes=[pltpu.VMEM((n, R, NY), jnp.float32), pltpu.VMEM((R, NY), jnp.float32), pltpu.SemaphoreType.DMA((n,)), pltpu.SemaphoreType.DMA(())],
        name="finish_last", compiler_params=pltpu.CompilerParams(vmem_limit_bytes=4 << 20),
    )(*parts, before)


def wave_tools(where, G, NB):
    me_g = where[0]
    kk, lane = iotas()
    left_edge, right_edge = lane == 0, lane == LANES - 1
    g = me_g ^ off_of(kk)
    up_idx, dn_idx = (at_off(me_g ^ ((g + step) & 7)) for step in (-1, 1))
    has_up, has_dn = g > 0, g < SUB - 1

    def halos(buf):
        for c in range(4):
            for b in range(NB):
                v = buf[c, G, :, cut(b)]
                buf[c, 0, :, cut(b)] = jnp.where(has_up, jnp.take_along_axis(v, up_idx, axis=0), 0.0)
                v = buf[c, 1, :, cut(b)]
                buf[c, G + 1, :, cut(b)] = jnp.where(has_dn, jnp.take_along_axis(v, dn_idx, axis=0), 0.0)

    def around(up, mid, dn):
        r = [a + b for a, b in zip(up, dn)]
        t = [m + 0.25 * a for m, a in zip(mid, r)]
        left = [jnp.where(left_edge, 0.0, pltpu.roll(t[-1], 1, 1))] + t[:-1]
        right = t[1:] + [jnp.where(right_edge, 0.0, pltpu.roll(t[0], LANES - 1, 1))]
        return [a + (b + c) for a, b, c in zip(r, left, right)]

    def sweep(src_buf, put, base, count, done=None):
        def body(j, _):
            i0 = base + j * U1
            for f in range(2):
                rows = [[[src_buf[2 * f + c, i0 + q, :, cut(b)] for b in range(NB)] for q in range(U1 + 2)] for c in range(2)]
                for q in range(U1):
                    o = [around(rows[c][q], rows[c][q + 1], rows[c][q + 2]) for c in range(2)]
                    put(f, q, i0 + q, o, [rows[c][q + 1] for c in range(2)])
            if done is not None:
                done(i0)
            return 0

        lax.fori_loop(0, count // U1, body, 0)

    return halos, sweep


def times(mod, i, b, x, y):
    br, bi = mod[0, i, :, cut(b)], mod[1, i, :, cut(b)]
    return br * x - bi * y, br * y + bi * x


def first_kernel(cfg, where, om_ref, *refs):
    metas, R = cfg["metas"], cfg["R"]
    blks, (*cur, sh, e1, mod) = refs[: len(metas)], refs[len(metas) :]
    G, NB = mod.shape[1], mod.shape[3] // LANES
    lo = where[1]
    bases = [lo * R, (1 - lo) * R][: G // R]
    places = [[None] * SUB for _ in bases]
    for ref, (k0, kb, half, first) in zip(blks, metas):
        for k in range(kb):
            places[half][k0 + k] = (ref, first + k)
    halos, sweep = wave_tools(where, G, NB)
    om = om_ref[0]
    k1 = 6.0 / om
    kp = 0.01 * om

    def cell(i, b, v, eta):
        cf = (v * k1) * (1.0 + 2.0 * eta)
        d = cf * (10.0 / 3.0)
        den = 1.0 + d * d
        inv = 1.0 / (v * den)
        ph = kp * (den * inv)
        bi = (cf * (2.0 / 3.0)) * (v * inv)
        mod[0, i, :, cut(b)] = bi * d
        mod[1, i, :, cut(b)] = bi
        z = ph * ph
        sn = ph * horner(SIN_C, z)
        cs = horner(COS_C, z)
        for f in range(2):
            re, im = cur[f][0, i, :, cut(b)], cur[f][1, i, :, cut(b)]
            sh[2 * f, i + 1, :, cut(b)] = re * cs - im * sn
            sh[2 * f + 1, i + 1, :, cut(b)] = im * cs + re * sn

    for half, base in enumerate(bases):
        def stage0(j, _):
            rows = pl.ds(pl.multiple_of(j * SUB, SUB), SUB)
            for b in range(NB):
                v, eta = (turn([ref[k, m, rows, cut(b)] for ref, k in places[half]]) for m in range(2))
                for q in range(SUB):
                    cell(base + j * SUB + q, b, v[q], eta[q])
            return 0

        lax.fori_loop(0, R // SUB, stage0, 0)
    halos(sh)

    def put(f, q, i, o, mid):
        for b in range(NB):
            x, y = times(mod, i, b, o[0][b] - 5.0 * mid[0][b], o[1][b] - 5.0 * mid[1][b])
            e1[2 * f, i + 1, :, cut(b)] = x
            e1[2 * f + 1, i + 1, :, cut(b)] = y

    sweep(sh, put, 0, G)
    halos(e1)


def second_kernel(cfg, where, sh, e1, mod, *refs):
    last, R = cfg["last"], cfg["R"]
    G, NB = mod.shape[1], mod.shape[3] // LANES
    outs, refs = refs[: G // R], list(refs[G // R :])
    lo = where[1]
    bases = [lo * R, (1 - lo) * R][: G // R]
    st, (e2, *keep) = (None, refs) if last else (refs[:2], refs[2:])
    halos, sweep = wave_tools(where, G, NB)

    def put2(f, q, i, o, mid):
        for b in range(NB):
            x, y = times(mod, i, b, o[0][b], o[1][b])
            e2[2 * f, i + 1, :, cut(b)] = x
            e2[2 * f + 1, i + 1, :, cut(b)] = y

    sweep(e1, put2, 0, G)
    halos(e2)

    def put3(f, q, i, o, mid):
        for b in range(NB):
            x, y = times(mod, i, b, o[0][b], o[1][b])
            new = []
            for c, x in enumerate((x, y)):
                total = (x + mid[c][b]) + e1[2 * f + c, i + 1, :, cut(b)]
                new.append(sh[2 * f + c, i + 1, :, cut(b)] + (total + total))
                if not last:
                    st[f][c, i, :, cut(b)] = new[c]
                elif f == 0:
                    keep[0][c, q, :, cut(b)] = new[c]
            if f == 1:
                sr, si = (keep[0][c, q, :, cut(b)] if last else st[0][c, i, :, cut(b)] for c in range(2))
                images[b][q] = sr * new[0] - si * new[1]

    images = [[None] * SUB for _ in range(NB)]
    for o_i in reversed(range(len(outs))):
        def send(i0):
            rows = pl.ds(pl.multiple_of(i0 - bases[o_i], SUB), SUB)
            for b in range(NB):
                for k, v in enumerate(turn(images[b])):
                    outs[o_i][k, rows, cut(b)] = v

        sweep(e2, put3, bases[o_i], R, send)


def first_call(where, omega, blocks, metas, state, R):
    _, G, _, NY = state[0].shape
    smem, vmem, _ = spaces()
    pad = jax.ShapeDtypeStruct((4, G + 2, SUB, NY), jnp.float32)
    return pl.pallas_call(
        lambda *r: first_kernel(dict(metas=metas, R=R), *r), out_shape=[pad, pad, jax.ShapeDtypeStruct((2, G, SUB, NY), jnp.float32)],
        in_specs=[smem, smem] + [vmem] * (len(blocks) + 2), out_specs=[vmem] * 3, name="first_half",
        compiler_params=pltpu.CompilerParams(vmem_limit_bytes=VLIM),
    )(where, omega, *blocks, *state)


def second_call(where, sh, e1, mod, last, R):
    _, G, _, NY = mod.shape
    smem, vmem, _ = spaces()
    out_shape = [jax.ShapeDtypeStruct((SUB, R, NY), jnp.float32)] * (G // R)
    out_specs = [vmem] * (G // R)
    if not last:
        out_shape += [jax.ShapeDtypeStruct((2, G, SUB, NY), jnp.float32)] * 2
        out_specs += [vmem] * 2
    scratch = [pltpu.VMEM((4, G + 2, SUB, NY), jnp.float32)]
    if last:
        scratch.append(pltpu.VMEM((2, U1, SUB, NY), jnp.float32))
    return pl.pallas_call(
        lambda *r: second_kernel(dict(last=last, R=R), *r), out_shape=out_shape,
        in_specs=[smem] + [vmem] * 3, out_specs=out_specs,
        scratch_shapes=scratch, name="second_half",
        compiler_params=pltpu.CompilerParams(vmem_limit_bytes=VLIM),
    )(where, sh, e1, mod)


HALF = SUB // 2


def swap(x, mask):
    n = lax.axis_size("freq")
    return lax.ppermute(x, "freq", [(i, i ^ mask) for i in range(n)])


def exchange_path(source, receiver, velocity, anisotropy, omega, scale):
    me = lax.axis_index("freq")
    depth_count, R, _ = velocity.shape
    G = R * lax.axis_size("freq") // SUB
    where = jnp.stack([me >> 1, me & 1]).astype(jnp.int32)
    own = list(prep_models(velocity, anisotropy, (0,), False))
    *rest, all_own = prep_models(velocity, anisotropy, tuple(range(1, depth_count)), True)
    own += rest
    state = [prep_field(where, source, 0, 1.0, G)]
    state.append(prep_field(where, receiver, 0, -1.0, G))
    all_near = swap(all_own, 2)
    shared = [all_own, all_near, swap(all_own, 1), swap(all_near, 1)]
    corners = [(0, 0), (HALF, 0), (0, 1), (HALF, 1)]
    sums = []
    for d in range(depth_count):
        last = d == depth_count - 1
        parts = [swap(own[d], far << 2) for far in range(1, HALF)]
        mine = jnp.stack(parts)
        near = swap(mine, 2)
        blocks = shared + [mine, near, swap(mine, 1), swap(near, 1)]
        metas = [(k0, 1, half, d) for k0, half in corners] + [(k0 + 1, HALF - 1, half, 0) for k0, half in corners]
        mid = first_call(where, omega, blocks, metas, state, R)
        kept, sent, *state = second_call(where, *mid, last, R)
        got = swap(sent, 1)
        upper = kept[HALF:] + got[HALF:]
        sums.append((kept, got, swap(upper, 2)))

    def z_sum(chosen):
        many = [[(k[far] + g[far]) + n[far] for k, g, n in chosen] for far in range(HALF)]
        parts = [x[0] if len(x) == 1 else jnp.stack(x) for x in many]
        return [parts[0]] + [swap(parts[far], far << 2) for far in range(1, HALF)]

    early = z_sum(sums[:-2])
    middle = z_sum(sums[-2:-1])
    tail = z_sum(sums[-1:])
    before = finish_early(scale, jnp.concatenate([sum(early[1:], early[0]), sum(middle[1:], middle[0])[None]]))
    return finish_last(scale, tail, before)


def apart(x):
    nb = x.shape[-1] // LANES
    return jnp.swapaxes(x.reshape(x.shape[:-1] + (LANES, nb)), -1, -2).reshape(x.shape)


def together(x):
    nb = x.shape[-1] // LANES
    return jnp.swapaxes(x.reshape(x.shape[:-1] + (nb, LANES)), -1, -2).reshape(x.shape)


def gather_path(source, receiver, velocity, anisotropy, omega, scale):
    depth_count = velocity.shape[0]
    both = lax.all_gather(apart(jnp.stack([velocity, anisotropy], axis=1)), "freq", axis=2, tiled=True)
    NX, NY = both.shape[2:]
    G = NX // SUB
    places = [off_of(k) for k in range(SUB)]
    back = [places.index(g) for g in range(SUB)]
    both = both.reshape(depth_count, 2, SUB, G, NY)
    both = jnp.stack([both[:, :, g] for g in places], axis=1)
    where = jnp.zeros((2,), jnp.int32)
    states = [[prep_field(where, source, p, 1.0, G), prep_field(where, receiver, p, -1.0, G)] for p in range(source.shape[0])]
    layers = []
    for d in range(depth_count):
        total = None
        for p, state in enumerate(states):
            last = d == depth_count - 1
            mid = first_call(where, omega[p : p + 1], [both[d]], [(0, SUB, 0, 0)], state, G)
            res = second_call(where, *mid, last, G)
            total = res[0] if total is None else total + res[0]
            states[p] = None if last else res[1:]
        whole = jnp.concatenate([total[k] for k in back], axis=0)
        layers.append(lax.psum_scatter(whole, "freq", scatter_dimension=0, tiled=True))
    return together(jnp.stack(layers)) * scale


def use_exchange(n, rows, pairs, depth):
    return n == 2 * SUB and rows % SUB == 0 and pairs == 1 and depth == 4


def on_device(source, receiver, velocity, anisotropy, frequency):
    pair_count = source.shape[0]
    n = lax.axis_size("freq")
    freq_total = frequency.shape[0]
    pair_ids = lax.axis_index("freq") * pair_count + jnp.arange(pair_count, dtype=jnp.int32)
    lookup = pair_ids[:, None] % freq_total == jnp.arange(freq_total, dtype=jnp.int32)[None, :]
    omega = jnp.sum(jnp.where(lookup, frequency[None, :], 0.0), axis=1)
    exchange = use_exchange(n, velocity.shape[1], pair_count, velocity.shape[0])
    path = exchange_path if exchange else gather_path
    return path(source, receiver, velocity, anisotropy, omega, 1.0 / math.sqrt(pair_count * n))


def solution(mesh):
    in_specs = (
        P(("survey", "freq"), None, None, None),
        P(("survey", "freq"), None, None, None),
        P("survey", "freq", None),
        P("survey", "freq", None),
        P(),
    )
    out_specs = P("survey", "freq", None)
    return jax.shard_map(
        on_device, mesh=mesh, in_specs=in_specs, out_specs=out_specs, check_vma=False
    )
```

```python
import math
import numpy as np
import jax
import jax.numpy as jnp
from jax import lax
from jax.experimental import pallas as pl
from jax.experimental.pallas import tpu as pltpu
from jax.sharding import PartitionSpec as P


LANES = 128
SUB = 8
U1 = SUB
VLIM = 28 << 20
TOP = 1.7


def even_fit(fun, degree):
    top = TOP * TOP
    nodes = 0.5 * top * (1.0 + np.cos(np.pi * (np.arange(degree + 1) + 0.5) / (degree + 1)))
    return [float(c) for c in np.polynomial.polynomial.polyfit(nodes, fun(np.sqrt(nodes)), degree)]


SIN_C = even_fit(lambda x: np.sin(x) / x, 4)
COS_C = even_fit(np.cos, 5)


def horner(coefs, z):
    acc = z * coefs[-1] + coefs[-2]
    for c in coefs[-3::-1]:
        acc = acc * z + c
    return acc


def off_of(k):
    return ((k & 3) << 1) | (k >> 2)


def at_off(o):
    return ((o & 1) << 2) | (o >> 1)


def cut(b):
    return slice(b * LANES, (b + 1) * LANES)


def iotas():
    return (lax.broadcasted_iota(jnp.int32, (SUB, LANES), 0), lax.broadcasted_iota(jnp.int32, (SUB, LANES), 1))


def pick(parts, which, index):
    out = jnp.take_along_axis(parts[0], index, axis=1)
    for a in range(1, len(parts)):
        out = jnp.where(which == a, jnp.take_along_axis(parts[a], index, axis=1), out)
    return out


def spread(parts):
    nb, lane = len(parts), iotas()[1]
    w = LANES // nb
    place = lane // w
    sorted_parts = [
        jnp.take_along_axis(x, (lane % w) * nb + (place + (nb - a)) % nb, axis=1) for a, x in enumerate(parts)
    ]
    out = []
    for b in range(nb):
        mixed = sorted_parts[0]
        for a in range(1, nb):
            mixed = jnp.where(place == (a + b) % nb, sorted_parts[a], mixed)
        out.append(pltpu.roll(mixed, LANES - w * b, 1) if b else mixed)
    return out


def turn(v):
    sub = iotas()[0]
    v = list(v)
    step = SUB // 2
    while step:
        low = (sub & step) == 0
        for a in range(SUB):
            if a & step == 0:
                x, y = v[a], v[a + step]
                v[a] = jnp.where(low, x, pltpu.roll(y, step, 0))
                v[a + step] = jnp.where(low, pltpu.roll(x, SUB - step, 0), y)
        step //= 2
    return v


def gather_back(parts):
    nb, lane = len(parts), iotas()[1]
    return [pick(parts, lane % nb, lane // nb + a * (LANES // nb)) for a in range(nb)]


def spaces():
    return [pl.BlockSpec(memory_space=s) for s in (pltpu.SMEM, pltpu.VMEM, pltpu.HBM)]


def prep_first_kernel(both, out):
    _, R, NY = both.shape
    nb = NY // LANES
    for m in range(2):
        for j in range(R // SUB):
            rows = slice(j * SUB, (j + 1) * SUB)
            for b, v in enumerate(spread([both[m, rows, cut(b)] for b in range(nb)])):
                out[m, rows, cut(b)] = v


def prep_first(both):
    return pl.pallas_call(
        prep_first_kernel, out_shape=jax.ShapeDtypeStruct(both.shape, jnp.float32), name="prep_first",
        compiler_params=pltpu.CompilerParams(vmem_limit_bytes=4 << 20),
    )(both)


def prep_models_kernel(groups, vel, ani, *outs):
    depth, R, NY = vel.shape
    nb = NY // LANES

    def body(j, _):
        rows = pl.ds(pl.multiple_of(j * SUB, SUB), SUB)
        for d in range(depth):
            for m, ref in enumerate((vel, ani)):
                for b, v in enumerate(spread([ref[d, rows, cut(b)] for b in range(nb)])):
                    for group, out in zip(groups, outs):
                        if d in group:
                            out[group.index(d), m, rows, cut(b)] = v
        return 0

    lax.fori_loop(0, R // SUB, body, 0)


def prep_models(vel, ani, groups):
    _, R, NY = vel.shape
    _, vmem, _ = spaces()
    return pl.pallas_call(
        lambda *r: prep_models_kernel(groups, *r), out_shape=[jax.ShapeDtypeStruct((len(g), 2, R, NY), jnp.float32) for g in groups],
        in_specs=[vmem] * 2, out_specs=[vmem] * len(groups),
        name="prep_models", compiler_params=pltpu.CompilerParams(vmem_limit_bytes=4 << 20),
    )(vel, ani)


def prep_field_kernel(p, sign, where, field, out):
    G, NY = out.shape[1], out.shape[3]
    nb = NY // LANES
    starts = [(where[0] ^ off_of(k)) * G for k in range(SUB)]

    def body(j, _):
        for c in range(2):
            cols = []
            for b in range(nb):
                rows = [field[p, c, pl.ds(pl.multiple_of(starts[k] + j * SUB, SUB), SUB), cut(b)] for k in range(SUB)]
                cols.append(turn(rows))
            for q in range(SUB):
                new = spread([cols[b][q] for b in range(nb)])
                for b in range(nb):
                    out[c, j * SUB + q, :, cut(b)] = -new[b] if c == 1 and sign < 0 else new[b]
        return 0

    lax.fori_loop(0, G // SUB, body, 0)


def prep_field(where, field, p, sign, G):
    NY = field.shape[-1]
    shape = (2, G, SUB, NY)
    smem, vmem, _ = spaces()
    return pl.pallas_call(
        lambda *r: prep_field_kernel(p, sign, *r), out_shape=jax.ShapeDtypeStruct(shape, jnp.float32), in_specs=[smem, vmem], out_specs=vmem, name="prep_field",
        compiler_params=pltpu.CompilerParams(vmem_limit_bytes=12 << 20),
    )(where, field)


def finish_early_kernel(scale, early, out, buf, sem):
    depth, R, NY = early.shape
    nb = NY // LANES
    for d in range(depth):
        for j in range(R // SUB):
            rows = slice(j * SUB, (j + 1) * SUB)
            new = gather_back([early[d, rows, cut(b)] * scale for b in range(nb)])
            for b in range(nb):
                buf[d, rows, cut(b)] = new[b]
    copy = pltpu.make_async_copy(buf, out.at[pl.ds(0, depth)], sem)
    copy.start()
    copy.wait()


def finish_early(scale, early):
    depth, R, NY = early.shape
    _, vmem, hbm = spaces()
    return pl.pallas_call(
        lambda *r: finish_early_kernel(scale, *r),
        out_shape=jax.ShapeDtypeStruct((depth + 1, R, NY), jnp.float32), in_specs=[vmem], out_specs=hbm,
        scratch_shapes=[pltpu.VMEM((depth, R, NY), jnp.float32), pltpu.SemaphoreType.DMA(())], name="finish_early",
        compiler_params=pltpu.CompilerParams(vmem_limit_bytes=4 << 20),
    )(early)


def finish_last_kernel(scale, own, *refs):
    far, (before, out, got, buf, sem, sem_o) = refs[:-6], refs[-6:]
    R, NY = buf.shape
    nb = NY // LANES
    copies = [pltpu.make_async_copy(ref, got.at[n], sem.at[n]) for n, ref in enumerate((own, *far))]
    for c in copies:
        c.start()
    for c in copies:
        c.wait()
    for j in range(R // SUB):
        rows = slice(j * SUB, (j + 1) * SUB)
        parts = []
        for b in range(nb):
            v = got[0, rows, cut(b)]
            for n in range(1, got.shape[0]):
                v = v + got[n, rows, cut(b)]
            parts.append(v * scale)
        new = gather_back(parts)
        for b in range(nb):
            buf[rows, cut(b)] = new[b]
    last = pltpu.make_async_copy(buf, out.at[out.shape[0] - 1], sem_o)
    last.start()
    last.wait()


def finish_last(scale, parts, before):
    R, NY = parts[0].shape
    _, _, hbm = spaces()
    n = len(parts)
    return pl.pallas_call(
        lambda *r: finish_last_kernel(scale, *r), out_shape=jax.ShapeDtypeStruct(before.shape, jnp.float32),
        in_specs=[hbm] * (n + 1), out_specs=hbm, input_output_aliases={n: 0},
        scratch_shapes=[pltpu.VMEM((n, R, NY), jnp.float32), pltpu.VMEM((R, NY), jnp.float32), pltpu.SemaphoreType.DMA((n,)), pltpu.SemaphoreType.DMA(())],
        name="finish_last", compiler_params=pltpu.CompilerParams(vmem_limit_bytes=4 << 20),
    )(*parts, before)


def wave_tools(where, G, NB):
    me_g = where[0]
    kk, lane = iotas()
    left_edge, right_edge = lane == 0, lane == LANES - 1
    g = me_g ^ off_of(kk)
    up_idx, dn_idx = (at_off(me_g ^ ((g + step) & 7)) for step in (-1, 1))
    has_up, has_dn = g > 0, g < SUB - 1

    def halos(buf):
        for c in range(4):
            for b in range(NB):
                v = buf[c, G, :, cut(b)]
                buf[c, 0, :, cut(b)] = jnp.where(has_up, jnp.take_along_axis(v, up_idx, axis=0), 0.0)
                v = buf[c, 1, :, cut(b)]
                buf[c, G + 1, :, cut(b)] = jnp.where(has_dn, jnp.take_along_axis(v, dn_idx, axis=0), 0.0)

    def around(up, mid, dn):
        r = [a + b for a, b in zip(up, dn)]
        t = [m + 0.25 * a for m, a in zip(mid, r)]
        left = [jnp.where(left_edge, 0.0, pltpu.roll(t[-1], 1, 1))] + t[:-1]
        right = t[1:] + [jnp.where(right_edge, 0.0, pltpu.roll(t[0], LANES - 1, 1))]
        return [a + (b + c) for a, b, c in zip(r, left, right)]

    def sweep(src_buf, put, base, count, done=None):
        def body(j, _):
            i0 = base + j * U1
            for f in range(2):
                rows = [[[src_buf[2 * f + c, i0 + q, :, cut(b)] for b in range(NB)] for q in range(U1 + 2)] for c in range(2)]
                for q in range(U1):
                    o = [around(rows[c][q], rows[c][q + 1], rows[c][q + 2]) for c in range(2)]
                    put(f, q, i0 + q, o, [rows[c][q + 1] for c in range(2)])
            if done is not None:
                done(i0)
            return 0

        lax.fori_loop(0, count // U1, body, 0)

    return halos, sweep


def times(mod, i, b, x, y):
    br, bi = mod[0, i, :, cut(b)], mod[1, i, :, cut(b)]
    return br * x - bi * y, br * y + bi * x


def first_kernel(cfg, where, om_ref, *refs):
    metas, R = cfg["metas"], cfg["R"]
    blks, (*cur, sh, e1, mod) = refs[: len(metas)], refs[len(metas) :]
    G, NB = mod.shape[1], mod.shape[3] // LANES
    lo = where[1]
    bases = [lo * R, (1 - lo) * R][: G // R]
    places = [[None] * SUB for _ in bases]
    for ref, (k0, kb, half, first) in zip(blks, metas):
        for k in range(kb):
            places[half][k0 + k] = (ref, first + k)
    halos, sweep = wave_tools(where, G, NB)
    om = om_ref[where[2]]
    k1 = 6.0 / om
    kp = 0.01 * om

    def cell(i, b, v, eta):
        cf = (v * k1) * (1.0 + 2.0 * eta)
        d = cf * (10.0 / 3.0)
        den = 1.0 + d * d
        inv = 1.0 / (v * den)
        ph = kp * (den * inv)
        bi = (cf * (2.0 / 3.0)) * (v * inv)
        mod[0, i, :, cut(b)] = bi * d
        mod[1, i, :, cut(b)] = bi
        z = ph * ph
        sn = ph * horner(SIN_C, z)
        cs = horner(COS_C, z)
        for f in range(2):
            re, im = cur[f][0, i, :, cut(b)], cur[f][1, i, :, cut(b)]
            sh[2 * f, i + 1, :, cut(b)] = re * cs - im * sn
            sh[2 * f + 1, i + 1, :, cut(b)] = im * cs + re * sn

    for half, base in enumerate(bases):
        def stage0(j, _):
            rows = pl.ds(pl.multiple_of(j * SUB, SUB), SUB)
            for b in range(NB):
                v, eta = (turn([ref[k, m, rows, cut(b)] for ref, k in places[half]]) for m in range(2))
                for q in range(SUB):
                    cell(base + j * SUB + q, b, v[q], eta[q])
            return 0

        lax.fori_loop(0, R // SUB, stage0, 0)
    halos(sh)

    def put(f, q, i, o, mid):
        for b in range(NB):
            x, y = times(mod, i, b, o[0][b] - 5.0 * mid[0][b], o[1][b] - 5.0 * mid[1][b])
            e1[2 * f, i + 1, :, cut(b)] = x
            e1[2 * f + 1, i + 1, :, cut(b)] = y

    sweep(sh, put, 0, G)
    halos(e1)


def second_kernel(cfg, where, sh, e1, mod, *refs):
    last, R = cfg["last"], cfg["R"]
    G, NB = mod.shape[1], mod.shape[3] // LANES
    outs, refs = refs[: G // R], list(refs[G // R :])
    lo = where[1]
    bases = [lo * R, (1 - lo) * R][: G // R]
    st, (e2, *keep) = (None, refs) if last else (refs[:2], refs[2:])
    halos, sweep = wave_tools(where, G, NB)

    def put2(f, q, i, o, mid):
        for b in range(NB):
            x, y = times(mod, i, b, o[0][b], o[1][b])
            e2[2 * f, i + 1, :, cut(b)] = x
            e2[2 * f + 1, i + 1, :, cut(b)] = y

    sweep(e1, put2, 0, G)
    halos(e2)

    def put3(f, q, i, o, mid):
        for b in range(NB):
            x, y = times(mod, i, b, o[0][b], o[1][b])
            new = []
            for c, x in enumerate((x, y)):
                total = (x + mid[c][b]) + e1[2 * f + c, i + 1, :, cut(b)]
                new.append(sh[2 * f + c, i + 1, :, cut(b)] + (total + total))
                if not last:
                    st[f][c, i, :, cut(b)] = new[c]
                elif f == 0:
                    keep[0][c, q, :, cut(b)] = new[c]
            if f == 1:
                sr, si = (keep[0][c, q, :, cut(b)] if last else st[0][c, i, :, cut(b)] for c in range(2))
                images[b][q] = sr * new[0] - si * new[1]

    images = [[None] * SUB for _ in range(NB)]
    for o_i in reversed(range(len(outs))):
        def send(i0):
            rows = pl.ds(pl.multiple_of(i0 - bases[o_i], SUB), SUB)
            for b in range(NB):
                for k, v in enumerate(turn(images[b])):
                    outs[o_i][k, rows, cut(b)] = v

        sweep(e2, put3, bases[o_i], R, send)


def first_call(where, frequency, blocks, metas, state, R):
    _, G, _, NY = state[0].shape
    smem, vmem, _ = spaces()
    pad = jax.ShapeDtypeStruct((4, G + 2, SUB, NY), jnp.float32)
    return pl.pallas_call(
        lambda *r: first_kernel(dict(metas=metas, R=R), *r), out_shape=[pad, pad, jax.ShapeDtypeStruct((2, G, SUB, NY), jnp.float32)],
        in_specs=[smem, smem] + [vmem] * (len(blocks) + 2), out_specs=[vmem] * 3, name="first_half",
        compiler_params=pltpu.CompilerParams(vmem_limit_bytes=VLIM),
    )(where, frequency, *blocks, *state)


def second_call(where, sh, e1, mod, last, R):
    _, G, _, NY = mod.shape
    smem, vmem, _ = spaces()
    out_shape = [jax.ShapeDtypeStruct((SUB, R, NY), jnp.float32)] * (G // R)
    out_specs = [vmem] * (G // R)
    if not last:
        out_shape += [jax.ShapeDtypeStruct((2, G, SUB, NY), jnp.float32)] * 2
        out_specs += [vmem] * 2
    scratch = [pltpu.VMEM((4, G + 2, SUB, NY), jnp.float32)]
    if last:
        scratch.append(pltpu.VMEM((2, U1, SUB, NY), jnp.float32))
    return pl.pallas_call(
        lambda *r: second_kernel(dict(last=last, R=R), *r), out_shape=out_shape,
        in_specs=[smem] + [vmem] * 3, out_specs=out_specs,
        scratch_shapes=scratch, name="second_half",
        compiler_params=pltpu.CompilerParams(vmem_limit_bytes=VLIM),
    )(where, sh, e1, mod)


HALF = SUB // 2


def swap(x, mask):
    n = lax.axis_size("freq")
    return lax.ppermute(x, "freq", [(i, i ^ mask) for i in range(n)])


def exchange_path(source, receiver, velocity, anisotropy, frequency, scale):
    me = lax.axis_index("freq")
    depth_count, R, _ = velocity.shape
    G = R * lax.axis_size("freq") // SUB
    where = jnp.stack([me >> 1, me & 1, lax.rem(me, frequency.shape[0])]).astype(jnp.int32)
    first = jnp.stack([velocity[0], anisotropy[0]])
    own = [prep_first(first)[None]]
    groups = ((1,), tuple(range(2, depth_count)), tuple(range(depth_count)))
    *rest, all_own = prep_models(velocity, anisotropy, groups)
    own += rest
    state = [prep_field(where, source, 0, 1.0, G)]
    state.append(prep_field(where, receiver, 0, -1.0, G))
    all_near = swap(all_own, 2)
    shared = [all_own, all_near, swap(all_own, 1), swap(all_near, 1)]
    corners = [(0, 0), (HALF, 0), (0, 1), (HALF, 1)]
    sums = []
    for d in range(depth_count):
        last = d == depth_count - 1
        if d < len(own):
            come = [swap(own[d], far << 2) for far in range(1, HALF)]
        parts = [x[max(0, d - 2)] for x in come]
        mine = jnp.stack(parts)
        near = swap(mine, 2)
        blocks = shared + [mine, near, swap(mine, 1), swap(near, 1)]
        metas = [(k0, 1, half, d) for k0, half in corners] + [(k0 + 1, HALF - 1, half, 0) for k0, half in corners]
        mid = first_call(where, frequency, blocks, metas, state, R)
        kept, sent, *state = second_call(where, *mid, last, R)
        got = swap(sent, 1)
        upper = kept[HALF:] + got[HALF:]
        sums.append((kept, got, swap(upper, 2)))

    def z_sum(chosen):
        many = [[(k[far] + g[far]) + n[far] for k, g, n in chosen] for far in range(HALF)]
        parts = [x[0] if len(x) == 1 else jnp.stack(x) for x in many]
        return [parts[0]] + [swap(parts[far], far << 2) for far in range(1, HALF)]

    early = z_sum(sums[:-2])
    middle = z_sum(sums[-2:-1])
    tail = z_sum(sums[-1:])
    before = jnp.concatenate([sum(early[1:], early[0]), sum(middle[1:], middle[0])[None]])
    before = finish_early(scale, before)
    return finish_last(scale, tail, before)


def apart(x):
    nb = x.shape[-1] // LANES
    return jnp.swapaxes(x.reshape(x.shape[:-1] + (LANES, nb)), -1, -2).reshape(x.shape)


def together(x):
    nb = x.shape[-1] // LANES
    return jnp.swapaxes(x.reshape(x.shape[:-1] + (nb, LANES)), -1, -2).reshape(x.shape)


def gather_path(source, receiver, velocity, anisotropy, frequency, scale):
    depth_count = velocity.shape[0]
    both = lax.all_gather(apart(jnp.stack([velocity, anisotropy], axis=1)), "freq", axis=2, tiled=True)
    NX, NY = both.shape[2:]
    G = NX // SUB
    places = [off_of(k) for k in range(SUB)]
    back = [places.index(g) for g in range(SUB)]
    both = both.reshape(depth_count, 2, SUB, G, NY)
    both = jnp.stack([both[:, :, g] for g in places], axis=1)
    pairs = source.shape[0]
    ids = lax.axis_index("freq") * pairs + jnp.arange(pairs, dtype=jnp.int32)
    wheres = [jnp.stack([0 * i, 0 * i, lax.rem(i, frequency.shape[0])]).astype(jnp.int32) for i in ids]
    states = [[prep_field(wheres[p], source, p, 1.0, G), prep_field(wheres[p], receiver, p, -1.0, G)] for p in range(pairs)]
    layers = []
    for d in range(depth_count):
        total = None
        for p, state in enumerate(states):
            last = d == depth_count - 1
            mid = first_call(wheres[p], frequency, [both[d]], [(0, SUB, 0, 0)], state, G)
            res = second_call(wheres[p], *mid, last, G)
            total = res[0] if total is None else total + res[0]
            states[p] = None if last else res[1:]
        whole = jnp.concatenate([total[k] for k in back], axis=0)
        layers.append(lax.psum_scatter(whole, "freq", scatter_dimension=0, tiled=True))
    return together(jnp.stack(layers)) * scale


def use_exchange(n, rows, pairs, depth):
    return n == 2 * SUB and rows % SUB == 0 and pairs == 1 and depth == 4


def on_device(source, receiver, velocity, anisotropy, frequency):
    pair_count = source.shape[0]
    n = lax.axis_size("freq")
    exchange = use_exchange(n, velocity.shape[1], pair_count, velocity.shape[0])
    path = exchange_path if exchange else gather_path
    return path(source, receiver, velocity, anisotropy, frequency, 1.0 / math.sqrt(pair_count * n))


def solution(mesh):
    in_specs = (
        P(("survey", "freq"), None, None, None),
        P(("survey", "freq"), None, None, None),
        P("survey", "freq", None),
        P("survey", "freq", None),
        P(),
    )
    out_specs = P("survey", "freq", None)
    return jax.shard_map(
        on_device, mesh=mesh, in_specs=in_specs, out_specs=out_specs, check_vma=False
    )
```

```python
import math
import numpy as np
import jax
import jax.numpy as jnp
from jax import lax
from jax.experimental import pallas as pl
from jax.experimental.pallas import tpu as pltpu
from jax.sharding import PartitionSpec as P


LANES = 128
SUB = 8
U1 = SUB
VLIM = 28 << 20
TOP = 1.7


def even_fit(fun, degree):
    top = TOP * TOP
    nodes = 0.5 * top * (1.0 + np.cos(np.pi * (np.arange(degree + 1) + 0.5) / (degree + 1)))
    return [float(c) for c in np.polynomial.polynomial.polyfit(nodes, fun(np.sqrt(nodes)), degree)]


SIN_C = even_fit(lambda x: np.sin(x) / x, 4)
COS_C = even_fit(np.cos, 5)


def horner(coefs, z):
    acc = z * coefs[-1] + coefs[-2]
    for c in coefs[-3::-1]:
        acc = acc * z + c
    return acc


def off_of(k):
    return ((k & 3) << 1) | (k >> 2)


def at_off(o):
    return ((o & 1) << 2) | (o >> 1)


def cut(b):
    return slice(b * LANES, (b + 1) * LANES)


def iotas():
    return (lax.broadcasted_iota(jnp.int32, (SUB, LANES), 0), lax.broadcasted_iota(jnp.int32, (SUB, LANES), 1))


def pick(parts, which, index):
    out = jnp.take_along_axis(parts[0], index, axis=1)
    for a in range(1, len(parts)):
        out = jnp.where(which == a, jnp.take_along_axis(parts[a], index, axis=1), out)
    return out


def spread(parts):
    nb, lane = len(parts), iotas()[1]
    w = LANES // nb
    place = lane // w
    sorted_parts = [
        jnp.take_along_axis(x, (lane % w) * nb + (place + (nb - a)) % nb, axis=1) for a, x in enumerate(parts)
    ]
    out = []
    for b in range(nb):
        mixed = sorted_parts[0]
        for a in range(1, nb):
            mixed = jnp.where(place == (a + b) % nb, sorted_parts[a], mixed)
        out.append(pltpu.roll(mixed, LANES - w * b, 1) if b else mixed)
    return out


def turn(v):
    sub = iotas()[0]
    v = list(v)
    step = SUB // 2
    while step:
        low = (sub & step) == 0
        for a in range(SUB):
            if a & step == 0:
                x, y = v[a], v[a + step]
                v[a] = jnp.where(low, x, pltpu.roll(y, step, 0))
                v[a + step] = jnp.where(low, pltpu.roll(x, SUB - step, 0), y)
        step //= 2
    return v


def gather_back(parts):
    nb, lane = len(parts), iotas()[1]
    return [pick(parts, lane % nb, lane // nb + a * (LANES // nb)) for a in range(nb)]


def spaces():
    return [pl.BlockSpec(memory_space=s) for s in (pltpu.SMEM, pltpu.VMEM, pltpu.HBM)]


def prep_models_kernel(both, *outs):
    depth, _, R, NY = both.shape
    nb = NY // LANES

    def body(j, _):
        rows = pl.ds(pl.multiple_of(j * SUB, SUB), SUB)
        for d in range(depth):
            for m in range(2):
                for b, v in enumerate(spread([both[d, m, rows, cut(b)] for b in range(nb)])):
                    outs[d][m, rows, cut(b)] = v
                    outs[depth][d, m, rows, cut(b)] = v
        return 0

    lax.fori_loop(0, R // SUB, body, 0)


def prep_models(both):
    return pl.pallas_call(
        prep_models_kernel, out_shape=[jax.ShapeDtypeStruct(x, jnp.float32) for x in [both.shape[1:]] * both.shape[0] + [both.shape]],
        name="prep_models", compiler_params=pltpu.CompilerParams(vmem_limit_bytes=4 << 20),
        cost_estimate=pl.CostEstimate(flops=1 << 24, transcendentals=0, bytes_accessed=1 << 24),
    )(both)


def prep_field_kernel(p, sign, where, field, out):
    G, NY = out.shape[1], out.shape[3]
    nb = NY // LANES
    starts = [(where[0] ^ off_of(k)) * G for k in range(SUB)]

    def body(j, _):
        for c in range(2):
            cols = []
            for b in range(nb):
                rows = [field[p, c, pl.ds(pl.multiple_of(starts[k] + j * SUB, SUB), SUB), cut(b)] for k in range(SUB)]
                cols.append(turn(rows))
            for q in range(SUB):
                new = spread([cols[b][q] for b in range(nb)])
                for b in range(nb):
                    out[c, j * SUB + q, :, cut(b)] = -new[b] if c == 1 and sign < 0 else new[b]
        return 0

    lax.fori_loop(0, G // SUB, body, 0)


def prep_field(where, field, p, sign, G):
    NY = field.shape[-1]
    shape = (2, G, SUB, NY)
    smem, vmem, _ = spaces()
    return pl.pallas_call(
        lambda *r: prep_field_kernel(p, sign, *r), out_shape=jax.ShapeDtypeStruct(shape, jnp.float32), in_specs=[smem, vmem], out_specs=vmem, name="prep_field",
        compiler_params=pltpu.CompilerParams(vmem_limit_bytes=12 << 20),
    )(where, field)


def finish_early_kernel(scale, early, out, buf, sem):
    depth, R, NY = early.shape
    nb = NY // LANES
    for d in range(depth):
        for j in range(R // SUB):
            rows = slice(j * SUB, (j + 1) * SUB)
            new = gather_back([early[d, rows, cut(b)] * scale for b in range(nb)])
            for b in range(nb):
                buf[d, rows, cut(b)] = new[b]
    copy = pltpu.make_async_copy(buf, out.at[pl.ds(0, depth)], sem)
    copy.start()
    copy.wait()


def finish_early(scale, early):
    depth, R, NY = early.shape
    _, vmem, hbm = spaces()
    return pl.pallas_call(
        lambda *r: finish_early_kernel(scale, *r),
        out_shape=jax.ShapeDtypeStruct((depth + 1, R, NY), jnp.float32), in_specs=[vmem], out_specs=hbm,
        scratch_shapes=[pltpu.VMEM((depth, R, NY), jnp.float32), pltpu.SemaphoreType.DMA(())], name="finish_early",
        compiler_params=pltpu.CompilerParams(vmem_limit_bytes=4 << 20),
    )(early)


def finish_last_kernel(scale, own, *refs):
    far, (before, out, got, buf, sem, sem_o) = refs[:-6], refs[-6:]
    R, NY = buf.shape
    nb = NY // LANES
    copies = [pltpu.make_async_copy(ref, got.at[n], sem.at[n]) for n, ref in enumerate((own, *far))]
    for c in copies:
        c.start()
    for c in copies:
        c.wait()
    for j in range(R // SUB):
        rows = slice(j * SUB, (j + 1) * SUB)
        parts = []
        for b in range(nb):
            v = got[0, rows, cut(b)]
            for n in range(1, got.shape[0]):
                v = v + got[n, rows, cut(b)]
            parts.append(v * scale)
        new = gather_back(parts)
        for b in range(nb):
            buf[rows, cut(b)] = new[b]
    last = pltpu.make_async_copy(buf, out.at[out.shape[0] - 1], sem_o)
    last.start()
    last.wait()


def finish_last(scale, parts, before):
    R, NY = parts[0].shape
    _, _, hbm = spaces()
    n = len(parts)
    return pl.pallas_call(
        lambda *r: finish_last_kernel(scale, *r), out_shape=jax.ShapeDtypeStruct(before.shape, jnp.float32),
        in_specs=[hbm] * (n + 1), out_specs=hbm, input_output_aliases={n: 0},
        scratch_shapes=[pltpu.VMEM((n, R, NY), jnp.float32), pltpu.VMEM((R, NY), jnp.float32), pltpu.SemaphoreType.DMA((n,)), pltpu.SemaphoreType.DMA(())],
        name="finish_last", compiler_params=pltpu.CompilerParams(vmem_limit_bytes=4 << 20),
    )(*parts, before)


def wave_tools(where, G, NB):
    me_g = where[0]
    kk, lane = iotas()
    left_edge, right_edge = lane == 0, lane == LANES - 1
    g = me_g ^ off_of(kk)
    up_idx, dn_idx = (at_off(me_g ^ ((g + step) & 7)) for step in (-1, 1))
    has_up, has_dn = g > 0, g < SUB - 1

    def halos(buf):
        for c in range(4):
            for b in range(NB):
                v = buf[c, G, :, cut(b)]
                buf[c, 0, :, cut(b)] = jnp.where(has_up, jnp.take_along_axis(v, up_idx, axis=0), 0.0)
                v = buf[c, 1, :, cut(b)]
                buf[c, G + 1, :, cut(b)] = jnp.where(has_dn, jnp.take_along_axis(v, dn_idx, axis=0), 0.0)

    def around(up, mid, dn):
        r = [a + b for a, b in zip(up, dn)]
        t = [m + 0.25 * a for m, a in zip(mid, r)]
        left = [jnp.where(left_edge, 0.0, pltpu.roll(t[-1], 1, 1))] + t[:-1]
        right = t[1:] + [jnp.where(right_edge, 0.0, pltpu.roll(t[0], LANES - 1, 1))]
        return [a + (b + c) for a, b, c in zip(r, left, right)]

    def sweep(src_buf, put, base, count, done=None):
        def body(j, _):
            i0 = base + j * U1
            for f in range(2):
                rows = [[[src_buf[2 * f + c, i0 + q, :, cut(b)] for b in range(NB)] for q in range(U1 + 2)] for c in range(2)]
                for q in range(U1):
                    o = [around(rows[c][q], rows[c][q + 1], rows[c][q + 2]) for c in range(2)]
                    put(f, q, i0 + q, o, [rows[c][q + 1] for c in range(2)])
            if done is not None:
                done(i0)
            return 0

        lax.fori_loop(0, count // U1, body, 0)

    return halos, sweep


def times(mod, i, b, x, y):
    br, bi = mod[0, i, :, cut(b)], mod[1, i, :, cut(b)]
    return br * x - bi * y, br * y + bi * x


def first_kernel(cfg, where, om_ref, *refs):
    metas, R = cfg["metas"], cfg["R"]
    blks, (*cur, sh, e1, mod) = refs[: len(metas)], refs[len(metas) :]
    G, NB = mod.shape[1], mod.shape[3] // LANES
    lo = where[1]
    bases = [lo * R, (1 - lo) * R][: G // R]
    places = [[None] * SUB for _ in bases]
    for ref, (k0, kb, half, first) in zip(blks, metas):
        for k in range(kb):
            places[half][k0 + k] = (ref, first + k)
    halos, sweep = wave_tools(where, G, NB)
    om = om_ref[where[2]]
    k1 = 6.0 / om
    kp = 0.01 * om

    def cell(i, b, v, eta):
        cf = (v * k1) * (1.0 + 2.0 * eta)
        d = cf * (10.0 / 3.0)
        den = 1.0 + d * d
        inv = 1.0 / (v * den)
        ph = kp * (den * inv)
        bi = (cf * (2.0 / 3.0)) * (v * inv)
        mod[0, i, :, cut(b)] = bi * d
        mod[1, i, :, cut(b)] = bi
        z = ph * ph
        sn = ph * horner(SIN_C, z)
        cs = horner(COS_C, z)
        for f in range(2):
            re, im = cur[f][0, i, :, cut(b)], cur[f][1, i, :, cut(b)]
            sh[2 * f, i + 1, :, cut(b)] = re * cs - im * sn
            sh[2 * f + 1, i + 1, :, cut(b)] = im * cs + re * sn

    for half, base in enumerate(bases):
        def stage0(j, _):
            rows = pl.ds(pl.multiple_of(j * SUB, SUB), SUB)
            for b in range(NB):
                v, eta = (turn([ref[k, m, rows, cut(b)] for ref, k in places[half]]) for m in range(2))
                for q in range(SUB):
                    cell(base + j * SUB + q, b, v[q], eta[q])
            return 0

        lax.fori_loop(0, R // SUB, stage0, 0)
    halos(sh)

    def put(f, q, i, o, mid):
        for b in range(NB):
            x, y = times(mod, i, b, o[0][b] - 5.0 * mid[0][b], o[1][b] - 5.0 * mid[1][b])
            e1[2 * f, i + 1, :, cut(b)] = x
            e1[2 * f + 1, i + 1, :, cut(b)] = y

    sweep(sh, put, 0, G)
    halos(e1)


def second_kernel(cfg, where, sh, e1, mod, *refs):
    last, R, part = cfg["last"], cfg["R"], cfg["part"]
    G, NB = mod.shape[1], mod.shape[3] // LANES
    lo = where[1]
    bases = [lo * R, (1 - lo) * R][: G // R]
    refs = list(refs)
    e2 = refs.pop(0) if part == "kept" else None
    chosen = {"sent": [1], "kept": [0], None: list(range(len(bases)))}[part]
    outs = {o_i: refs.pop(0) for o_i in chosen}
    st = None if last else (refs.pop(0), refs.pop(0))
    e2 = refs.pop(0) if e2 is None else e2
    keep = refs
    halos, sweep = wave_tools(where, G, NB)

    def put2(f, q, i, o, mid):
        for b in range(NB):
            x, y = times(mod, i, b, o[0][b], o[1][b])
            e2[2 * f, i + 1, :, cut(b)] = x
            e2[2 * f + 1, i + 1, :, cut(b)] = y

    if part != "kept":
        sweep(e1, put2, 0, G)
        halos(e2)

    def put3(f, q, i, o, mid):
        for b in range(NB):
            x, y = times(mod, i, b, o[0][b], o[1][b])
            new = []
            for c, x in enumerate((x, y)):
                total = (x + mid[c][b]) + e1[2 * f + c, i + 1, :, cut(b)]
                new.append(sh[2 * f + c, i + 1, :, cut(b)] + (total + total))
                if not last:
                    st[f][c, i, :, cut(b)] = new[c]
                elif f == 0:
                    keep[0][c, q, :, cut(b)] = new[c]
            if f == 1:
                sr, si = (keep[0][c, q, :, cut(b)] if last else st[0][c, i, :, cut(b)] for c in range(2))
                images[b][q] = sr * new[0] - si * new[1]

    images = [[None] * SUB for _ in range(NB)]
    for o_i in reversed(chosen):
        def send(i0):
            rows = pl.ds(pl.multiple_of(i0 - bases[o_i], SUB), SUB)
            for b in range(NB):
                for k, v in enumerate(turn(images[b])):
                    outs[o_i][k, rows, cut(b)] = v

        sweep(e2, put3, bases[o_i], R, send)


def first_call(where, frequency, blocks, metas, state, R):
    _, G, _, NY = state[0].shape
    smem, vmem, _ = spaces()
    pad = jax.ShapeDtypeStruct((4, G + 2, SUB, NY), jnp.float32)
    return pl.pallas_call(
        lambda *r: first_kernel(dict(metas=metas, R=R), *r), out_shape=[pad, pad, jax.ShapeDtypeStruct((2, G, SUB, NY), jnp.float32)],
        in_specs=[smem, smem] + [vmem] * (len(blocks) + 2), out_specs=[vmem] * 3, name="first_half",
        compiler_params=pltpu.CompilerParams(vmem_limit_bytes=VLIM),
    )(where, frequency, *blocks, *state)


def second_call(where, sh, e1, mod, last, R, part=None, e2=None):
    _, G, _, NY = mod.shape
    smem, vmem, _ = spaces()
    count = G // R if part is None else 1
    out_shape = [jax.ShapeDtypeStruct((SUB, R, NY), jnp.float32)] * count
    pad = (4, G + 2, SUB, NY)
    scratch = []
    if not last:
        out_shape += [jax.ShapeDtypeStruct((2, G, SUB, NY), jnp.float32)] * 2
    if part == "sent":
        out_shape.append(jax.ShapeDtypeStruct(pad, jnp.float32))
    elif part is None:
        scratch.append(pltpu.VMEM(pad, jnp.float32))
    if last:
        scratch.append(pltpu.VMEM((2, U1, SUB, NY), jnp.float32))
    ins = [sh, e1, mod] + ([e2] if part == "kept" else [])
    return pl.pallas_call(
        lambda *r: second_kernel(dict(last=last, R=R, part=part), *r), out_shape=out_shape,
        in_specs=[smem] + [vmem] * len(ins), out_specs=[vmem] * len(out_shape),
        scratch_shapes=scratch,
        compiler_params=pltpu.CompilerParams(vmem_limit_bytes=VLIM),
    )(where, *ins)


HALF = SUB // 2


def swap(x, mask):
    n = lax.axis_size("freq")
    return lax.ppermute(x, "freq", [(i, i ^ mask) for i in range(n)])


def exchange_path(source, receiver, velocity, anisotropy, frequency, scale):
    me = lax.axis_index("freq")
    depth_count, R, _ = velocity.shape
    G = R * lax.axis_size("freq") // SUB
    where = jnp.stack([me >> 1, me & 1, lax.rem(me, frequency.shape[0])]).astype(jnp.int32)
    both = jnp.stack([velocity, anisotropy], axis=1)
    *own, all_own = prep_models(both)
    state = [prep_field(where, source, 0, 1.0, G)]
    state.append(prep_field(where, receiver, 0, -1.0, G))
    all_near = swap(all_own, 2)
    shared = [all_own, all_near, swap(all_own, 1), swap(all_near, 1)]
    corners = [(0, 0), (HALF, 0), (0, 1), (HALF, 1)]
    pieces = []
    for d in range(depth_count):
        last = d == depth_count - 1
        parts = [swap(own[d], far << 2) for far in range(1, HALF)]
        mine = jnp.stack(parts)
        near = swap(mine, 2)
        blocks = shared + [mine, near, swap(mine, 1), swap(near, 1)]
        metas = [(k0, 1, half, d) for k0, half in corners] + [(k0 + 1, HALF - 1, half, 0) for k0, half in corners]
        mid = first_call(where, frequency, blocks, metas, state, R)
        if last:
            sent, e2 = second_call(where, *mid, last, R, "sent")
            (kept,) = second_call(where, *mid, last, R, "kept", e2)
        else:
            kept, sent, *state = second_call(where, *mid, last, R)
        pieces.append((kept, swap(sent, 1)))

    def upper(d):
        return pieces[d][0][HALF:] + pieces[d][1][HALF:]

    def sums_of(depths):
        uppers = [upper(d) for d in depths]
        uppers = uppers[0] if len(depths) == 1 else jnp.stack(uppers)
        near = swap(uppers, 2)
        nears = [near] if len(depths) == 1 else [near[i] for i in range(len(depths))]
        many = [[(pieces[d][0][far] + pieces[d][1][far]) + n[far] for d, n in zip(depths, nears)] for far in range(HALF)]
        parts = [x[0] if len(x) == 1 else jnp.stack(x) for x in many]
        return [parts[0]] + [swap(parts[far], far << 2) for far in range(1, HALF)]

    early = sums_of([0])
    middle = sums_of(list(range(1, depth_count - 1)))
    tail = sums_of([depth_count - 1])
    before = jnp.concatenate([sum(early[1:], early[0])[None], sum(middle[1:], middle[0])])
    before = finish_early(scale, before)
    return finish_last(scale, tail, before)


def apart(x):
    nb = x.shape[-1] // LANES
    return jnp.swapaxes(x.reshape(x.shape[:-1] + (LANES, nb)), -1, -2).reshape(x.shape)


def together(x):
    nb = x.shape[-1] // LANES
    return jnp.swapaxes(x.reshape(x.shape[:-1] + (nb, LANES)), -1, -2).reshape(x.shape)


def gather_path(source, receiver, velocity, anisotropy, frequency, scale):
    depth_count = velocity.shape[0]
    both = lax.all_gather(apart(jnp.stack([velocity, anisotropy], axis=1)), "freq", axis=2, tiled=True)
    NX, NY = both.shape[2:]
    G = NX // SUB
    places = [off_of(k) for k in range(SUB)]
    back = [places.index(g) for g in range(SUB)]
    both = both.reshape(depth_count, 2, SUB, G, NY)
    both = jnp.stack([both[:, :, g] for g in places], axis=1)
    pairs = source.shape[0]
    ids = lax.axis_index("freq") * pairs + jnp.arange(pairs, dtype=jnp.int32)
    wheres = [jnp.stack([0 * i, 0 * i, lax.rem(i, frequency.shape[0])]).astype(jnp.int32) for i in ids]
    states = [[prep_field(wheres[p], source, p, 1.0, G), prep_field(wheres[p], receiver, p, -1.0, G)] for p in range(pairs)]
    layers = []
    for d in range(depth_count):
        total = None
        for p, state in enumerate(states):
            last = d == depth_count - 1
            mid = first_call(wheres[p], frequency, [both[d]], [(0, SUB, 0, 0)], state, G)
            res = second_call(wheres[p], *mid, last, G)
            total = res[0] if total is None else total + res[0]
            states[p] = None if last else res[1:]
        whole = jnp.concatenate([total[k] for k in back], axis=0)
        layers.append(lax.psum_scatter(whole, "freq", scatter_dimension=0, tiled=True))
    return together(jnp.stack(layers)) * scale


def use_exchange(n, rows, pairs, depth):
    return n == 2 * SUB and rows % SUB == 0 and pairs == 1 and depth == 4


def on_device(source, receiver, velocity, anisotropy, frequency):
    pair_count = source.shape[0]
    n = lax.axis_size("freq")
    exchange = use_exchange(n, velocity.shape[1], pair_count, velocity.shape[0])
    path = exchange_path if exchange else gather_path
    return path(source, receiver, velocity, anisotropy, frequency, 1.0 / math.sqrt(pair_count * n))


def solution(mesh):
    in_specs = (
        P(("survey", "freq"), None, None, None),
        P(("survey", "freq"), None, None, None),
        P("survey", "freq", None),
        P("survey", "freq", None),
        P(),
    )
    out_specs = P("survey", "freq", None)
    return jax.shard_map(
        on_device, mesh=mesh, in_specs=in_specs, out_specs=out_specs, check_vma=False
    )
```

```python
import math
import numpy as np
import jax
import jax.numpy as jnp
from jax import lax
from jax.experimental import pallas as pl
from jax.experimental.pallas import tpu as pltpu
from jax.sharding import PartitionSpec as P


LANES = 128
SUB = 8
U1 = SUB
VLIM = 28 << 20
TOP = 1.7


def even_fit(fun, degree):
    top = TOP * TOP
    nodes = 0.5 * top * (1.0 + np.cos(np.pi * (np.arange(degree + 1) + 0.5) / (degree + 1)))
    return [float(c) for c in np.polynomial.polynomial.polyfit(nodes, fun(np.sqrt(nodes)), degree)]


SIN_C = even_fit(lambda x: np.sin(x) / x, 4)
COS_C = even_fit(np.cos, 5)


def horner(coefs, z):
    acc = z * coefs[-1] + coefs[-2]
    for c in coefs[-3::-1]:
        acc = acc * z + c
    return acc


def off_of(k):
    return ((k & 3) << 1) | (k >> 2)


def at_off(o):
    return ((o & 1) << 2) | (o >> 1)


def cut(b):
    return slice(b * LANES, (b + 1) * LANES)


def iotas():
    return (lax.broadcasted_iota(jnp.int32, (SUB, LANES), 0), lax.broadcasted_iota(jnp.int32, (SUB, LANES), 1))


def pick(parts, which, index):
    out = jnp.take_along_axis(parts[0], index, axis=1)
    for a in range(1, len(parts)):
        out = jnp.where(which == a, jnp.take_along_axis(parts[a], index, axis=1), out)
    return out


def spread(parts):
    nb, lane = len(parts), iotas()[1]
    w = LANES // nb
    place = lane // w
    sorted_parts = [
        jnp.take_along_axis(x, (lane % w) * nb + (place + (nb - a)) % nb, axis=1) for a, x in enumerate(parts)
    ]
    out = []
    for b in range(nb):
        mixed = sorted_parts[0]
        for a in range(1, nb):
            mixed = jnp.where(place == (a + b) % nb, sorted_parts[a], mixed)
        out.append(pltpu.roll(mixed, LANES - w * b, 1) if b else mixed)
    return out


def turn(v):
    sub = iotas()[0]
    v = list(v)
    step = SUB // 2
    while step:
        low = (sub & step) == 0
        for a in range(SUB):
            if a & step == 0:
                x, y = v[a], v[a + step]
                v[a] = jnp.where(low, x, pltpu.roll(y, step, 0))
                v[a + step] = jnp.where(low, pltpu.roll(x, SUB - step, 0), y)
        step //= 2
    return v


def gather_back(parts):
    nb, lane = len(parts), iotas()[1]
    return [pick(parts, lane % nb, lane // nb + a * (LANES // nb)) for a in range(nb)]


def spaces():
    return [pl.BlockSpec(memory_space=s) for s in (pltpu.SMEM, pltpu.VMEM, pltpu.HBM)]


def prep_models_kernel(both, *outs):
    depth, _, R, NY = both.shape
    nb = NY // LANES

    def body(j, _):
        rows = pl.ds(pl.multiple_of(j * SUB, SUB), SUB)
        for d in range(depth):
            for m in range(2):
                for b, v in enumerate(spread([both[d, m, rows, cut(b)] for b in range(nb)])):
                    outs[d][m, rows, cut(b)] = v
                    outs[depth][d, m, rows, cut(b)] = v
        return 0

    lax.fori_loop(0, R // SUB, body, 0)


def prep_models(both):
    return pl.pallas_call(
        prep_models_kernel, out_shape=[jax.ShapeDtypeStruct(x, jnp.float32) for x in [both.shape[1:]] * both.shape[0] + [both.shape]],
        name="prep_models", compiler_params=pltpu.CompilerParams(vmem_limit_bytes=4 << 20),
        cost_estimate=pl.CostEstimate(flops=1 << 24, transcendentals=0, bytes_accessed=1 << 24),
    )(both)


def prep_field_kernel(p, sign, where, field, out):
    G, NY = out.shape[1], out.shape[3]
    nb = NY // LANES
    starts = [(where[0] ^ off_of(k)) * G for k in range(SUB)]

    def body(j, _):
        for c in range(2):
            cols = []
            for b in range(nb):
                rows = [field[p, c, pl.ds(pl.multiple_of(starts[k] + j * SUB, SUB), SUB), cut(b)] for k in range(SUB)]
                cols.append(turn(rows))
            for q in range(SUB):
                new = spread([cols[b][q] for b in range(nb)])
                for b in range(nb):
                    out[c, j * SUB + q, :, cut(b)] = -new[b] if c == 1 and sign < 0 else new[b]
        return 0

    lax.fori_loop(0, G // SUB, body, 0)


def prep_field(where, field, p, sign, G):
    NY = field.shape[-1]
    shape = (2, G, SUB, NY)
    smem, vmem, _ = spaces()
    return pl.pallas_call(
        lambda *r: prep_field_kernel(p, sign, *r), out_shape=jax.ShapeDtypeStruct(shape, jnp.float32), in_specs=[smem, vmem], out_specs=vmem, name="prep_field",
        compiler_params=pltpu.CompilerParams(vmem_limit_bytes=12 << 20),
    )(where, field)


def finish_early_kernel(scale, early, out, buf, sem):
    depth, R, NY = early.shape
    nb = NY // LANES
    for d in range(depth):
        for j in range(R // SUB):
            rows = slice(j * SUB, (j + 1) * SUB)
            new = gather_back([early[d, rows, cut(b)] * scale for b in range(nb)])
            for b in range(nb):
                buf[d, rows, cut(b)] = new[b]
    copy = pltpu.make_async_copy(buf, out.at[pl.ds(0, depth)], sem)
    copy.start()
    copy.wait()


def finish_early(scale, early):
    depth, R, NY = early.shape
    _, vmem, hbm = spaces()
    return pl.pallas_call(
        lambda *r: finish_early_kernel(scale, *r),
        out_shape=jax.ShapeDtypeStruct((depth + 1, R, NY), jnp.float32), in_specs=[vmem], out_specs=hbm,
        scratch_shapes=[pltpu.VMEM((depth, R, NY), jnp.float32), pltpu.SemaphoreType.DMA(())], name="finish_early",
        compiler_params=pltpu.CompilerParams(vmem_limit_bytes=4 << 20),
    )(early)


def finish_last_kernel(scale, own, *refs):
    far, (before, out, got, buf, sem, sem_o) = refs[:-6], refs[-6:]
    R, NY = buf.shape
    nb = NY // LANES
    copies = [pltpu.make_async_copy(ref, got.at[n], sem.at[n]) for n, ref in enumerate((own, *far))]
    for c in copies:
        c.start()
    for c in copies:
        c.wait()
    for j in range(R // SUB):
        rows = slice(j * SUB, (j + 1) * SUB)
        parts = []
        for b in range(nb):
            v = got[0, rows, cut(b)]
            for n in range(1, got.shape[0]):
                v = v + got[n, rows, cut(b)]
            parts.append(v * scale)
        new = gather_back(parts)
        for b in range(nb):
            buf[rows, cut(b)] = new[b]
    last = pltpu.make_async_copy(buf, out.at[out.shape[0] - 1], sem_o)
    last.start()
    last.wait()


def finish_last(scale, parts, before):
    R, NY = parts[0].shape
    _, _, hbm = spaces()
    n = len(parts)
    return pl.pallas_call(
        lambda *r: finish_last_kernel(scale, *r), out_shape=jax.ShapeDtypeStruct(before.shape, jnp.float32),
        in_specs=[hbm] * (n + 1), out_specs=hbm, input_output_aliases={n: 0},
        scratch_shapes=[pltpu.VMEM((n, R, NY), jnp.float32), pltpu.VMEM((R, NY), jnp.float32), pltpu.SemaphoreType.DMA((n,)), pltpu.SemaphoreType.DMA(())],
        name="finish_last", compiler_params=pltpu.CompilerParams(vmem_limit_bytes=4 << 20),
    )(*parts, before)


def wave_tools(where, G, NB):
    me_g = where[0]
    kk, lane = iotas()
    left_edge, right_edge = lane == 0, lane == LANES - 1
    g = me_g ^ off_of(kk)
    up_idx, dn_idx = (at_off(me_g ^ ((g + step) & 7)) for step in (-1, 1))
    has_up, has_dn = g > 0, g < SUB - 1

    def halos(buf):
        for c in range(4):
            for b in range(NB):
                v = buf[c, G, :, cut(b)]
                buf[c, 0, :, cut(b)] = jnp.where(has_up, jnp.take_along_axis(v, up_idx, axis=0), 0.0)
                v = buf[c, 1, :, cut(b)]
                buf[c, G + 1, :, cut(b)] = jnp.where(has_dn, jnp.take_along_axis(v, dn_idx, axis=0), 0.0)

    def around(up, mid, dn):
        r = [a + b for a, b in zip(up, dn)]
        t = [m + 0.25 * a for m, a in zip(mid, r)]
        left = [jnp.where(left_edge, 0.0, pltpu.roll(t[-1], 1, 1))] + t[:-1]
        right = t[1:] + [jnp.where(right_edge, 0.0, pltpu.roll(t[0], LANES - 1, 1))]
        return [a + (b + c) for a, b, c in zip(r, left, right)]

    def sweep(src_buf, put, base, count, done=None):
        def body(j, _):
            i0 = base + j * U1
            for f in range(2):
                rows = [[[src_buf[2 * f + c, i0 + q, :, cut(b)] for b in range(NB)] for q in range(U1 + 2)] for c in range(2)]
                for q in range(U1):
                    o = [around(rows[c][q], rows[c][q + 1], rows[c][q + 2]) for c in range(2)]
                    put(f, q, i0 + q, o, [rows[c][q + 1] for c in range(2)])
            if done is not None:
                done(i0)
            return 0

        lax.fori_loop(0, count // U1, body, 0)

    return halos, sweep


def times(mod, i, b, x, y):
    br, bi = mod[0, i, :, cut(b)], mod[1, i, :, cut(b)]
    return br * x - bi * y, br * y + bi * x


def first_kernel(cfg, where, om_ref, *refs):
    metas, R = cfg["metas"], cfg["R"]
    blks, (*cur, sh, e1, mod) = refs[: len(metas)], refs[len(metas) :]
    G, NB = mod.shape[1], mod.shape[3] // LANES
    lo = where[1]
    bases = [lo * R, (1 - lo) * R][: G // R]
    places = [[None] * SUB for _ in bases]
    for ref, (k0, kb, half, first) in zip(blks, metas):
        for k in range(kb):
            places[half][k0 + k] = (ref, first + k)
    halos, sweep = wave_tools(where, G, NB)
    om = om_ref[where[2]]
    k1 = 6.0 / om
    kp = 0.01 * om

    def cell(i, b, v, eta):
        cf = (v * k1) * (1.0 + 2.0 * eta)
        d = cf * (10.0 / 3.0)
        den = 1.0 + d * d
        inv = 1.0 / (v * den)
        ph = kp * (den * inv)
        bi = (cf * (2.0 / 3.0)) * (v * inv)
        mod[0, i, :, cut(b)] = bi * d
        mod[1, i, :, cut(b)] = bi
        z = ph * ph
        sn = ph * horner(SIN_C, z)
        cs = horner(COS_C, z)
        for f in range(2):
            re, im = cur[f][0, i, :, cut(b)], cur[f][1, i, :, cut(b)]
            sh[2 * f, i + 1, :, cut(b)] = re * cs - im * sn
            sh[2 * f + 1, i + 1, :, cut(b)] = im * cs + re * sn

    for half, base in enumerate(bases):
        def stage0(j, _):
            rows = pl.ds(pl.multiple_of(j * SUB, SUB), SUB)
            for b in range(NB):
                v, eta = (turn([ref[k, m, rows, cut(b)] for ref, k in places[half]]) for m in range(2))
                for q in range(SUB):
                    cell(base + j * SUB + q, b, v[q], eta[q])
            return 0

        lax.fori_loop(0, R // SUB, stage0, 0)
    halos(sh)

    def put(f, q, i, o, mid):
        for b in range(NB):
            x, y = times(mod, i, b, o[0][b] - 5.0 * mid[0][b], o[1][b] - 5.0 * mid[1][b])
            e1[2 * f, i + 1, :, cut(b)] = x
            e1[2 * f + 1, i + 1, :, cut(b)] = y

    sweep(sh, put, 0, G)
    halos(e1)


def second_kernel(cfg, where, sh, e1, mod, *refs):
    last, R, part = cfg["last"], cfg["R"], cfg["part"]
    G, NB = mod.shape[1], mod.shape[3] // LANES
    lo = where[1]
    bases = [lo * R, (1 - lo) * R][: G // R]
    refs = list(refs)
    e2 = refs.pop(0) if part == "kept" else None
    chosen = {"sent": [1], "kept": [0], None: list(range(len(bases)))}[part]
    outs = {o_i: refs.pop(0) for o_i in chosen}
    st = None if last else (refs.pop(0), refs.pop(0))
    e2 = refs.pop(0) if e2 is None else e2
    keep = refs
    halos, sweep = wave_tools(where, G, NB)

    def put2(f, q, i, o, mid):
        for b in range(NB):
            x, y = times(mod, i, b, o[0][b], o[1][b])
            e2[2 * f, i + 1, :, cut(b)] = x
            e2[2 * f + 1, i + 1, :, cut(b)] = y

    if part != "kept":
        sweep(e1, put2, 0, G)
        halos(e2)

    def put3(f, q, i, o, mid):
        for b in range(NB):
            x, y = times(mod, i, b, o[0][b], o[1][b])
            new = []
            for c, x in enumerate((x, y)):
                total = (x + mid[c][b]) + e1[2 * f + c, i + 1, :, cut(b)]
                new.append(sh[2 * f + c, i + 1, :, cut(b)] + (total + total))
                if not last:
                    st[f][c, i, :, cut(b)] = new[c]
                elif f == 0:
                    keep[0][c, q, :, cut(b)] = new[c]
            if f == 1:
                sr, si = (keep[0][c, q, :, cut(b)] if last else st[0][c, i, :, cut(b)] for c in range(2))
                images[b][q] = sr * new[0] - si * new[1]

    images = [[None] * SUB for _ in range(NB)]
    for o_i in reversed(chosen):
        def send(i0):
            rows = pl.ds(pl.multiple_of(i0 - bases[o_i], SUB), SUB)
            for b in range(NB):
                for k, v in enumerate(turn(images[b])):
                    outs[o_i][k, rows, cut(b)] = v

        sweep(e2, put3, bases[o_i], R, send)


def first_call(where, frequency, blocks, metas, state, R):
    _, G, _, NY = state[0].shape
    smem, vmem, _ = spaces()
    pad = jax.ShapeDtypeStruct((4, G + 2, SUB, NY), jnp.float32)
    return pl.pallas_call(
        lambda *r: first_kernel(dict(metas=metas, R=R), *r), out_shape=[pad, pad, jax.ShapeDtypeStruct((2, G, SUB, NY), jnp.float32)],
        in_specs=[smem, smem] + [vmem] * (len(blocks) + 2), out_specs=[vmem] * 3, name="first_half",
        compiler_params=pltpu.CompilerParams(vmem_limit_bytes=VLIM),
    )(where, frequency, *blocks, *state)


def second_call(where, sh, e1, mod, last, R, part=None, e2=None):
    _, G, _, NY = mod.shape
    smem, vmem, _ = spaces()
    count = G // R if part is None else 1
    out_shape = [jax.ShapeDtypeStruct((SUB, R, NY), jnp.float32)] * count
    pad = (4, G + 2, SUB, NY)
    scratch = []
    if not last:
        out_shape += [jax.ShapeDtypeStruct((2, G, SUB, NY), jnp.float32)] * 2
    if part == "sent":
        out_shape.append(jax.ShapeDtypeStruct(pad, jnp.float32))
    elif part is None:
        scratch.append(pltpu.VMEM(pad, jnp.float32))
    if last:
        scratch.append(pltpu.VMEM((2, U1, SUB, NY), jnp.float32))
    ins = [sh, e1, mod] + ([e2] if part == "kept" else [])
    return pl.pallas_call(
        lambda *r: second_kernel(dict(last=last, R=R, part=part), *r), out_shape=out_shape,
        in_specs=[smem] + [vmem] * len(ins), out_specs=[vmem] * len(out_shape),
        scratch_shapes=scratch,
        compiler_params=pltpu.CompilerParams(vmem_limit_bytes=VLIM),
    )(where, *ins)


HALF = SUB // 2


def swap(x, mask):
    n = lax.axis_size("freq")
    return lax.ppermute(x, "freq", [(i, i ^ mask) for i in range(n)])


def exchange_path(source, receiver, velocity, anisotropy, frequency, scale):
    me = lax.axis_index("freq")
    depth_count, R, _ = velocity.shape
    G = R * lax.axis_size("freq") // SUB
    where = jnp.stack([me >> 1, me & 1, lax.rem(me, frequency.shape[0])]).astype(jnp.int32)
    both = jnp.stack([velocity, anisotropy], axis=1)
    *own, all_own = prep_models(both)
    state = [prep_field(where, source, 0, 1.0, G)]
    state.append(prep_field(where, receiver, 0, -1.0, G))
    all_near = swap(all_own, 2)
    shared = [all_own, all_near, swap(all_own, 1), swap(all_near, 1)]
    corners = [(0, 0), (HALF, 0), (0, 1), (HALF, 1)]
    pieces = []
    for d in range(depth_count):
        last = d == depth_count - 1
        parts = [swap(own[d], far << 2) for far in range(1, HALF)]
        mine = jnp.stack(parts)
        near = swap(mine, 2)
        blocks = shared + [mine, near, swap(mine, 1), swap(near, 1)]
        metas = [(k0, 1, half, d) for k0, half in corners] + [(k0 + 1, HALF - 1, half, 0) for k0, half in corners]
        mid = first_call(where, frequency, blocks, metas, state, R)
        if last:
            sent, e2 = second_call(where, *mid, last, R, "sent")
            (kept,) = second_call(where, *mid, last, R, "kept", e2)
        else:
            kept, sent, *state = second_call(where, *mid, last, R)
        pieces.append((kept, swap(sent, 1)))

    def upper(d):
        return pieces[d][0][HALF:] + pieces[d][1][HALF:]

    sums = []
    for d in range(depth_count):
        up = upper(d)
        sums.append((*pieces[d], swap(up, 2)))

    def z_sum(depths):
        many = [[(k[far] + g[far]) + n[far] for k, g, n in (sums[d] for d in depths)] for far in range(HALF)]
        parts = [x[0] if len(x) == 1 else jnp.stack(x) for x in many]
        return [parts[0]] + [swap(parts[far], far << 2) for far in range(1, HALF)]

    early = z_sum(list(range(depth_count - 2)))
    middle = z_sum([depth_count - 2])
    tail = z_sum([depth_count - 1])
    before = jnp.concatenate([sum(early[1:], early[0]), sum(middle[1:], middle[0])[None]])
    before = finish_early(scale, before)
    return finish_last(scale, tail, before)


def apart(x):
    nb = x.shape[-1] // LANES
    return jnp.swapaxes(x.reshape(x.shape[:-1] + (LANES, nb)), -1, -2).reshape(x.shape)


def together(x):
    nb = x.shape[-1] // LANES
    return jnp.swapaxes(x.reshape(x.shape[:-1] + (nb, LANES)), -1, -2).reshape(x.shape)


def gather_path(source, receiver, velocity, anisotropy, frequency, scale):
    depth_count = velocity.shape[0]
    both = lax.all_gather(apart(jnp.stack([velocity, anisotropy], axis=1)), "freq", axis=2, tiled=True)
    NX, NY = both.shape[2:]
    G = NX // SUB
    places = [off_of(k) for k in range(SUB)]
    back = [places.index(g) for g in range(SUB)]
    both = both.reshape(depth_count, 2, SUB, G, NY)
    both = jnp.stack([both[:, :, g] for g in places], axis=1)
    pairs = source.shape[0]
    ids = lax.axis_index("freq") * pairs + jnp.arange(pairs, dtype=jnp.int32)
    wheres = [jnp.stack([0 * i, 0 * i, lax.rem(i, frequency.shape[0])]).astype(jnp.int32) for i in ids]
    states = [[prep_field(wheres[p], source, p, 1.0, G), prep_field(wheres[p], receiver, p, -1.0, G)] for p in range(pairs)]
    layers = []
    for d in range(depth_count):
        total = None
        for p, state in enumerate(states):
            last = d == depth_count - 1
            mid = first_call(wheres[p], frequency, [both[d]], [(0, SUB, 0, 0)], state, G)
            res = second_call(wheres[p], *mid, last, G)
            total = res[0] if total is None else total + res[0]
            states[p] = None if last else res[1:]
        whole = jnp.concatenate([total[k] for k in back], axis=0)
        layers.append(lax.psum_scatter(whole, "freq", scatter_dimension=0, tiled=True))
    return together(jnp.stack(layers)) * scale


def use_exchange(n, rows, pairs, depth):
    return n == 2 * SUB and rows % SUB == 0 and pairs == 1 and depth == 4


def on_device(source, receiver, velocity, anisotropy, frequency):
    pair_count = source.shape[0]
    n = lax.axis_size("freq")
    exchange = use_exchange(n, velocity.shape[1], pair_count, velocity.shape[0])
    path = exchange_path if exchange else gather_path
    return path(source, receiver, velocity, anisotropy, frequency, 1.0 / math.sqrt(pair_count * n))


def solution(mesh):
    in_specs = (
        P(("survey", "freq"), None, None, None),
        P(("survey", "freq"), None, None, None),
        P("survey", "freq", None),
        P("survey", "freq", None),
        P(),
    )
    out_specs = P("survey", "freq", None)
    return jax.shard_map(
        on_device, mesh=mesh, in_specs=in_specs, out_specs=out_specs, check_vma=False
    )
```

```python
import math
import numpy as np
import jax
import jax.numpy as jnp
from jax import lax
from jax.experimental import pallas as pl
from jax.experimental.pallas import tpu as pltpu
from jax.sharding import PartitionSpec as P


LANES = 128
SUB = 8
U1 = SUB
VLIM = 28 << 20
TOP = 1.7


def even_fit(fun, degree):
    top = TOP * TOP
    nodes = 0.5 * top * (1.0 + np.cos(np.pi * (np.arange(degree + 1) + 0.5) / (degree + 1)))
    return [float(c) for c in np.polynomial.polynomial.polyfit(nodes, fun(np.sqrt(nodes)), degree)]


SIN_C = even_fit(lambda x: np.sin(x) / x, 4)
COS_C = even_fit(np.cos, 5)


def horner(coefs, z):
    acc = z * coefs[-1] + coefs[-2]
    for c in coefs[-3::-1]:
        acc = acc * z + c
    return acc


def off_of(k):
    return ((k & 3) << 1) | (k >> 2)


def at_off(o):
    return ((o & 1) << 2) | (o >> 1)


def cut(b):
    return slice(b * LANES, (b + 1) * LANES)


def iotas():
    return (lax.broadcasted_iota(jnp.int32, (SUB, LANES), 0), lax.broadcasted_iota(jnp.int32, (SUB, LANES), 1))


def pick(parts, which, index):
    out = jnp.take_along_axis(parts[0], index, axis=1)
    for a in range(1, len(parts)):
        out = jnp.where(which == a, jnp.take_along_axis(parts[a], index, axis=1), out)
    return out


def spread(parts):
    nb, lane = len(parts), iotas()[1]
    w = LANES // nb
    place = lane // w
    sorted_parts = [
        jnp.take_along_axis(x, (lane % w) * nb + (place + (nb - a)) % nb, axis=1) for a, x in enumerate(parts)
    ]
    out = []
    for b in range(nb):
        mixed = sorted_parts[0]
        for a in range(1, nb):
            mixed = jnp.where(place == (a + b) % nb, sorted_parts[a], mixed)
        out.append(pltpu.roll(mixed, LANES - w * b, 1) if b else mixed)
    return out


def turn(v):
    sub = iotas()[0]
    v = list(v)
    step = SUB // 2
    while step:
        low = (sub & step) == 0
        for a in range(SUB):
            if a & step == 0:
                x, y = v[a], v[a + step]
                v[a] = jnp.where(low, x, pltpu.roll(y, step, 0))
                v[a + step] = jnp.where(low, pltpu.roll(x, SUB - step, 0), y)
        step //= 2
    return v


def gather_back(parts):
    nb, lane = len(parts), iotas()[1]
    return [pick(parts, lane % nb, lane // nb + a * (LANES // nb)) for a in range(nb)]


def spaces():
    return [pl.BlockSpec(memory_space=s) for s in (pltpu.SMEM, pltpu.VMEM, pltpu.HBM)]


def prep_models_kernel(both, *outs):
    depth, _, R, NY = both.shape
    nb = NY // LANES

    def body(j, _):
        rows = pl.ds(pl.multiple_of(j * SUB, SUB), SUB)
        for d in range(depth):
            for m in range(2):
                for b, v in enumerate(spread([both[d, m, rows, cut(b)] for b in range(nb)])):
                    outs[d][m, rows, cut(b)] = v
                    outs[depth][d, m, rows, cut(b)] = v
        return 0

    lax.fori_loop(0, R // SUB, body, 0)


def prep_models(both):
    return pl.pallas_call(
        prep_models_kernel, out_shape=[jax.ShapeDtypeStruct(x, jnp.float32) for x in [both.shape[1:]] * both.shape[0] + [both.shape]],
        name="prep_models", compiler_params=pltpu.CompilerParams(vmem_limit_bytes=4 << 20),
        cost_estimate=pl.CostEstimate(flops=1 << 24, transcendentals=0, bytes_accessed=1 << 24),
    )(both)


def prep_field_kernel(p, sign, where, field, out):
    G, NY = out.shape[1], out.shape[3]
    nb = NY // LANES
    starts = [(where[0] ^ off_of(k)) * G for k in range(SUB)]

    def body(j, _):
        for c in range(2):
            cols = []
            for b in range(nb):
                rows = [field[p, c, pl.ds(pl.multiple_of(starts[k] + j * SUB, SUB), SUB), cut(b)] for k in range(SUB)]
                cols.append(turn(rows))
            for q in range(SUB):
                new = spread([cols[b][q] for b in range(nb)])
                for b in range(nb):
                    out[c, j * SUB + q, :, cut(b)] = -new[b] if c == 1 and sign < 0 else new[b]
        return 0

    lax.fori_loop(0, G // SUB, body, 0)


def prep_field(where, field, p, sign, G):
    NY = field.shape[-1]
    shape = (2, G, SUB, NY)
    smem, vmem, _ = spaces()
    return pl.pallas_call(
        lambda *r: prep_field_kernel(p, sign, *r), out_shape=jax.ShapeDtypeStruct(shape, jnp.float32), in_specs=[smem, vmem], out_specs=vmem, name="prep_field",
        compiler_params=pltpu.CompilerParams(vmem_limit_bytes=12 << 20),
    )(where, field)


def finish_early_kernel(scale, early, out, buf, sem):
    depth, R, NY = early.shape
    nb = NY // LANES
    for d in range(depth):
        for j in range(R // SUB):
            rows = slice(j * SUB, (j + 1) * SUB)
            new = gather_back([early[d, rows, cut(b)] * scale for b in range(nb)])
            for b in range(nb):
                buf[d, rows, cut(b)] = new[b]
    copy = pltpu.make_async_copy(buf, out.at[pl.ds(0, depth)], sem)
    copy.start()
    copy.wait()


def finish_early(scale, early):
    depth, R, NY = early.shape
    _, vmem, hbm = spaces()
    return pl.pallas_call(
        lambda *r: finish_early_kernel(scale, *r),
        out_shape=jax.ShapeDtypeStruct((depth + 1, R, NY), jnp.float32), in_specs=[vmem], out_specs=hbm,
        scratch_shapes=[pltpu.VMEM((depth, R, NY), jnp.float32), pltpu.SemaphoreType.DMA(())], name="finish_early",
        compiler_params=pltpu.CompilerParams(vmem_limit_bytes=4 << 20),
    )(early)


def finish_last_kernel(scale, own, *refs):
    far, (before, out, got, buf, sem, sem_o) = refs[:-6], refs[-6:]
    R, NY = buf.shape
    nb = NY // LANES
    copies = [pltpu.make_async_copy(ref, got.at[n], sem.at[n]) for n, ref in enumerate((own, *far))]
    for c in copies:
        c.start()
    for c in copies:
        c.wait()
    for j in range(R // SUB):
        rows = slice(j * SUB, (j + 1) * SUB)
        parts = []
        for b in range(nb):
            v = got[0, rows, cut(b)]
            for n in range(1, got.shape[0]):
                v = v + got[n, rows, cut(b)]
            parts.append(v * scale)
        new = gather_back(parts)
        for b in range(nb):
            buf[rows, cut(b)] = new[b]
    last = pltpu.make_async_copy(buf, out.at[out.shape[0] - 1], sem_o)
    last.start()
    last.wait()


def finish_last(scale, parts, before):
    R, NY = parts[0].shape
    _, _, hbm = spaces()
    n = len(parts)
    return pl.pallas_call(
        lambda *r: finish_last_kernel(scale, *r), out_shape=jax.ShapeDtypeStruct(before.shape, jnp.float32),
        in_specs=[hbm] * (n + 1), out_specs=hbm, input_output_aliases={n: 0},
        scratch_shapes=[pltpu.VMEM((n, R, NY), jnp.float32), pltpu.VMEM((R, NY), jnp.float32), pltpu.SemaphoreType.DMA((n,)), pltpu.SemaphoreType.DMA(())],
        name="finish_last", compiler_params=pltpu.CompilerParams(vmem_limit_bytes=4 << 20),
    )(*parts, before)


def wave_tools(where, G, NB):
    me_g = where[0]
    kk, lane = iotas()
    left_edge, right_edge = lane == 0, lane == LANES - 1
    g = me_g ^ off_of(kk)
    up_idx, dn_idx = (at_off(me_g ^ ((g + step) & 7)) for step in (-1, 1))
    has_up, has_dn = g > 0, g < SUB - 1

    def halos(buf):
        for c in range(4):
            for b in range(NB):
                v = buf[c, G, :, cut(b)]
                buf[c, 0, :, cut(b)] = jnp.where(has_up, jnp.take_along_axis(v, up_idx, axis=0), 0.0)
                v = buf[c, 1, :, cut(b)]
                buf[c, G + 1, :, cut(b)] = jnp.where(has_dn, jnp.take_along_axis(v, dn_idx, axis=0), 0.0)

    def around(up, mid, dn):
        r = [a + b for a, b in zip(up, dn)]
        t = [m + 0.25 * a for m, a in zip(mid, r)]
        left = [jnp.where(left_edge, 0.0, pltpu.roll(t[-1], 1, 1))] + t[:-1]
        right = t[1:] + [jnp.where(right_edge, 0.0, pltpu.roll(t[0], LANES - 1, 1))]
        return [a + (b + c) for a, b, c in zip(r, left, right)]

    def sweep(src_buf, put, base, count, done=None):
        def body(j, _):
            i0 = base + j * U1
            for f in range(2):
                rows = [[[src_buf[2 * f + c, i0 + q, :, cut(b)] for b in range(NB)] for q in range(U1 + 2)] for c in range(2)]
                for q in range(U1):
                    o = [around(rows[c][q], rows[c][q + 1], rows[c][q + 2]) for c in range(2)]
                    put(f, q, i0 + q, o, [rows[c][q + 1] for c in range(2)])
            if done is not None:
                done(i0)
            return 0

        lax.fori_loop(0, count // U1, body, 0)

    return halos, sweep


def times(mod, i, b, x, y):
    br, bi = mod[0, i, :, cut(b)], mod[1, i, :, cut(b)]
    return br * x - bi * y, br * y + bi * x


def first_kernel(cfg, where, om_ref, *refs):
    metas, R = cfg["metas"], cfg["R"]
    blks, (*cur, sh, e1, mod) = refs[: len(metas)], refs[len(metas) :]
    G, NB = mod.shape[1], mod.shape[3] // LANES
    lo = where[1]
    bases = [lo * R, (1 - lo) * R][: G // R]
    places = [[None] * SUB for _ in bases]
    for ref, (k0, kb, half, first) in zip(blks, metas):
        for k in range(kb):
            places[half][k0 + k] = (ref, first + k)
    halos, sweep = wave_tools(where, G, NB)
    om = om_ref[where[2]]
    k1 = 6.0 / om
    kp = 0.01 * om

    def cell(i, b, v, eta):
        cf = (v * k1) * (1.0 + 2.0 * eta)
        d = cf * (10.0 / 3.0)
        den = 1.0 + d * d
        inv = 1.0 / (v * den)
        ph = kp * (den * inv)
        bi = (cf * (2.0 / 3.0)) * (v * inv)
        mod[0, i, :, cut(b)] = bi * d
        mod[1, i, :, cut(b)] = bi
        z = ph * ph
        sn = ph * horner(SIN_C, z)
        cs = horner(COS_C, z)
        for f in range(2):
            re, im = cur[f][0, i, :, cut(b)], cur[f][1, i, :, cut(b)]
            sh[2 * f, i + 1, :, cut(b)] = re * cs - im * sn
            sh[2 * f + 1, i + 1, :, cut(b)] = im * cs + re * sn

    for half, base in enumerate(bases):
        def stage0(j, _):
            rows = pl.ds(pl.multiple_of(j * SUB, SUB), SUB)
            for b in range(NB):
                v, eta = (turn([ref[k, m, rows, cut(b)] for ref, k in places[half]]) for m in range(2))
                for q in range(SUB):
                    cell(base + j * SUB + q, b, v[q], eta[q])
            return 0

        lax.fori_loop(0, R // SUB, stage0, 0)
    halos(sh)

    def put(f, q, i, o, mid):
        for b in range(NB):
            x, y = times(mod, i, b, o[0][b] - 5.0 * mid[0][b], o[1][b] - 5.0 * mid[1][b])
            e1[2 * f, i + 1, :, cut(b)] = x
            e1[2 * f + 1, i + 1, :, cut(b)] = y

    sweep(sh, put, 0, G)
    halos(e1)


def second_kernel(cfg, where, sh, e1, mod, *refs):
    last, R, part = cfg["last"], cfg["R"], cfg["part"]
    G, NB = mod.shape[1], mod.shape[3] // LANES
    lo = where[1]
    bases = [lo * R, (1 - lo) * R][: G // R]
    refs = list(refs)
    e2 = refs.pop(0) if part == "kept" else None
    chosen = {"sent": [1], "kept": [0], None: list(range(len(bases)))}[part]
    outs = {o_i: refs.pop(0) for o_i in chosen}
    st = None if last else (refs.pop(0), refs.pop(0))
    e2 = refs.pop(0) if e2 is None else e2
    keep = refs
    halos, sweep = wave_tools(where, G, NB)

    def put2(f, q, i, o, mid):
        for b in range(NB):
            x, y = times(mod, i, b, o[0][b], o[1][b])
            e2[2 * f, i + 1, :, cut(b)] = x
            e2[2 * f + 1, i + 1, :, cut(b)] = y

    if part != "kept":
        sweep(e1, put2, 0, G)
        halos(e2)

    def put3(f, q, i, o, mid):
        for b in range(NB):
            x, y = times(mod, i, b, o[0][b], o[1][b])
            new = []
            for c, x in enumerate((x, y)):
                total = (x + mid[c][b]) + e1[2 * f + c, i + 1, :, cut(b)]
                new.append(sh[2 * f + c, i + 1, :, cut(b)] + (total + total))
                if not last:
                    st[f][c, i, :, cut(b)] = new[c]
                elif f == 0:
                    keep[0][c, q, :, cut(b)] = new[c]
            if f == 1:
                sr, si = (keep[0][c, q, :, cut(b)] if last else st[0][c, i, :, cut(b)] for c in range(2))
                images[b][q] = sr * new[0] - si * new[1]

    images = [[None] * SUB for _ in range(NB)]
    for o_i in reversed(chosen):
        def send(i0):
            rows = pl.ds(pl.multiple_of(i0 - bases[o_i], SUB), SUB)
            for b in range(NB):
                for k, v in enumerate(turn(images[b])):
                    outs[o_i][k, rows, cut(b)] = v

        sweep(e2, put3, bases[o_i], R, send)


def first_call(where, frequency, blocks, metas, state, R):
    _, G, _, NY = state[0].shape
    smem, vmem, _ = spaces()
    pad = jax.ShapeDtypeStruct((4, G + 2, SUB, NY), jnp.float32)
    return pl.pallas_call(
        lambda *r: first_kernel(dict(metas=metas, R=R), *r), out_shape=[pad, pad, jax.ShapeDtypeStruct((2, G, SUB, NY), jnp.float32)],
        in_specs=[smem, smem] + [vmem] * (len(blocks) + 2), out_specs=[vmem] * 3, name="first_half",
        compiler_params=pltpu.CompilerParams(vmem_limit_bytes=VLIM),
    )(where, frequency, *blocks, *state)


def second_call(where, sh, e1, mod, last, R, part=None, e2=None):
    _, G, _, NY = mod.shape
    smem, vmem, _ = spaces()
    count = G // R if part is None else 1
    out_shape = [jax.ShapeDtypeStruct((SUB, R, NY), jnp.float32)] * count
    pad = (4, G + 2, SUB, NY)
    scratch = []
    if not last:
        out_shape += [jax.ShapeDtypeStruct((2, G, SUB, NY), jnp.float32)] * 2
    if part == "sent":
        out_shape.append(jax.ShapeDtypeStruct(pad, jnp.float32))
    elif part is None:
        scratch.append(pltpu.VMEM(pad, jnp.float32))
    if last:
        scratch.append(pltpu.VMEM((2, U1, SUB, NY), jnp.float32))
    ins = [sh, e1, mod] + ([e2] if part == "kept" else [])
    return pl.pallas_call(
        lambda *r: second_kernel(dict(last=last, R=R, part=part), *r), out_shape=out_shape,
        in_specs=[smem] + [vmem] * len(ins), out_specs=[vmem] * len(out_shape),
        scratch_shapes=scratch,
        compiler_params=pltpu.CompilerParams(vmem_limit_bytes=VLIM),
    )(where, *ins)


HALF = SUB // 2


def swap(x, mask):
    n = lax.axis_size("freq")
    return lax.ppermute(x, "freq", [(i, i ^ mask) for i in range(n)])


def exchange_path(source, receiver, velocity, anisotropy, frequency, scale):
    me = lax.axis_index("freq")
    depth_count, R, _ = velocity.shape
    G = R * lax.axis_size("freq") // SUB
    where = jnp.stack([me >> 1, me & 1, lax.rem(me, frequency.shape[0])]).astype(jnp.int32)
    both = jnp.stack([velocity, anisotropy], axis=1)
    *own, all_own = prep_models(both)
    state = [prep_field(where, source, 0, 1.0, G)]
    state.append(prep_field(where, receiver, 0, -1.0, G))
    all_near = swap(all_own, 2)
    shared = [all_own, all_near, swap(all_own, 1), swap(all_near, 1)]
    corners = [(0, 0), (HALF, 0), (0, 1), (HALF, 1)]
    pieces = []
    for d in range(depth_count):
        last = d == depth_count - 1
        parts = [swap(own[d], far << 2) for far in range(1, HALF)]
        mine = jnp.stack(parts)
        near = swap(mine, 2)
        blocks = shared + [mine, near, swap(mine, 1), swap(near, 1)]
        metas = [(k0, 1, half, d) for k0, half in corners] + [(k0 + 1, HALF - 1, half, 0) for k0, half in corners]
        mid = first_call(where, frequency, blocks, metas, state, R)
        if last:
            sent, e2 = second_call(where, *mid, last, R, "sent")
            (kept,) = second_call(where, *mid, last, R, "kept", e2)
        else:
            kept, sent, *state = second_call(where, *mid, last, R)
        pieces.append((kept, swap(sent, 1)))

    def upper(d):
        return pieces[d][0][HALF:] + pieces[d][1][HALF:]

    first_ones = depth_count - 2
    joined = jnp.stack([upper(d) for d in range(first_ones)])
    joined = swap(joined, 2)
    nears = [joined[d] for d in range(first_ones)] + [swap(upper(d), 2) for d in range(first_ones, depth_count)]
    sums = [(*p, n) for p, n in zip(pieces, nears)]

    def z_sum(chosen):
        many = [[(k[far] + g[far]) + n[far] for k, g, n in chosen] for far in range(HALF)]
        parts = [x[0] if len(x) == 1 else jnp.stack(x) for x in many]
        return [parts[0]] + [swap(parts[far], far << 2) for far in range(1, HALF)]

    early = z_sum(sums[:-2])
    middle = z_sum(sums[-2:-1])
    tail = z_sum(sums[-1:])
    before = jnp.concatenate([sum(early[1:], early[0]), sum(middle[1:], middle[0])[None]])
    before = finish_early(scale, before)
    return finish_last(scale, tail, before)


def apart(x):
    nb = x.shape[-1] // LANES
    return jnp.swapaxes(x.reshape(x.shape[:-1] + (LANES, nb)), -1, -2).reshape(x.shape)


def together(x):
    nb = x.shape[-1] // LANES
    return jnp.swapaxes(x.reshape(x.shape[:-1] + (nb, LANES)), -1, -2).reshape(x.shape)


def gather_path(source, receiver, velocity, anisotropy, frequency, scale):
    depth_count = velocity.shape[0]
    both = lax.all_gather(apart(jnp.stack([velocity, anisotropy], axis=1)), "freq", axis=2, tiled=True)
    NX, NY = both.shape[2:]
    G = NX // SUB
    places = [off_of(k) for k in range(SUB)]
    back = [places.index(g) for g in range(SUB)]
    both = both.reshape(depth_count, 2, SUB, G, NY)
    both = jnp.stack([both[:, :, g] for g in places], axis=1)
    pairs = source.shape[0]
    ids = lax.axis_index("freq") * pairs + jnp.arange(pairs, dtype=jnp.int32)
    wheres = [jnp.stack([0 * i, 0 * i, lax.rem(i, frequency.shape[0])]).astype(jnp.int32) for i in ids]
    states = [[prep_field(wheres[p], source, p, 1.0, G), prep_field(wheres[p], receiver, p, -1.0, G)] for p in range(pairs)]
    layers = []
    for d in range(depth_count):
        total = None
        for p, state in enumerate(states):
            last = d == depth_count - 1
            mid = first_call(wheres[p], frequency, [both[d]], [(0, SUB, 0, 0)], state, G)
            res = second_call(wheres[p], *mid, last, G)
            total = res[0] if total is None else total + res[0]
            states[p] = None if last else res[1:]
        whole = jnp.concatenate([total[k] for k in back], axis=0)
        layers.append(lax.psum_scatter(whole, "freq", scatter_dimension=0, tiled=True))
    return together(jnp.stack(layers)) * scale


def use_exchange(n, rows, pairs, depth):
    return n == 2 * SUB and rows % SUB == 0 and pairs == 1 and depth == 4


def on_device(source, receiver, velocity, anisotropy, frequency):
    pair_count = source.shape[0]
    n = lax.axis_size("freq")
    exchange = use_exchange(n, velocity.shape[1], pair_count, velocity.shape[0])
    path = exchange_path if exchange else gather_path
    return path(source, receiver, velocity, anisotropy, frequency, 1.0 / math.sqrt(pair_count * n))


def solution(mesh):
    in_specs = (
        P(("survey", "freq"), None, None, None),
        P(("survey", "freq"), None, None, None),
        P("survey", "freq", None),
        P("survey", "freq", None),
        P(),
    )
    out_specs = P("survey", "freq", None)
    return jax.shard_map(
        on_device, mesh=mesh, in_specs=in_specs, out_specs=out_specs, check_vma=False
    )
```
